256 devices in a mesh: rows: 32 (over y_lo, z, core), cols: 8 (over y_hi, x).
Axes of the slice: x: 4, y: 4 (y_hi: 2, y_lo: 2; y = y_hi * 2 + y_lo), z: 8, core: 2. Of those that a mesh axis runs over, the one named last changes fastest.
Arguments:
- features: bfloat16 [32, 1024, 256], P('rows', 'cols'), may hold values from -48 to 48
- projection: bfloat16 [256, 512], replicated, may hold values from -1 to 1
- first_kernel: bfloat16 [3, 3, 256, 128], replicated, may hold values from -0.125 to 0.125
- second_kernel: bfloat16 [3, 3, 128, 128], replicated, may hold values from -0.1875 to 0.1875
- cotangent: bfloat16 [32, 1024, 128], P('rows', 'cols'), may hold values from -6 to 6
Outputs:
- output_map: bfloat16 [32, 1024, 128], P('rows', 'cols')
- input_grad: bfloat16 [32, 1024, 256], P('rows', 'cols')
- projection_grad: float32 [256, 512], replicated
- first_grad: float32 [3, 3, 256, 128], replicated
- second_grad: float32 [3, 3, 128, 128], replicated
The draws below stay inside these ranges and needn't reach their ends.
All inputs are finite; a program needn't handle non-finite values.
Results may differ from the reference program's by a relative error of at most 0.033.
Values may be sent and summed in bfloat16 or wider, within the bound.
A program may use at most 64 MiB of HBM per device.

```python
import math
import jax
import jax.numpy as jnp
from jax import lax

CH = 256
QK = 128
VAL = 256
HEADS = 8
CONV = 128
HEIGHT = 32
WIDTH = 1024


def draw_features(key, part):
    keys_all = jax.random.split(key, 1)
    result = jnp.clip(jax.random.normal(keys_all[0], (HEIGHT, WIDTH, CH), jnp.float32), -4.5, 4.5)
    return result.astype(jnp.bfloat16)


def draw_projection(key, part):
    keys_all = jax.random.split(key, 3)
    base = jnp.clip(jax.random.normal(keys_all[0], (CH, QK), jnp.float32), -4.5, 4.5)
    other = jnp.clip(jax.random.normal(keys_all[1], (CH, QK), jnp.float32), -4.5, 4.5)
    values_part = jnp.clip(jax.random.normal(keys_all[2], (CH, VAL), jnp.float32), -4.5, 4.5)
    result = jnp.concatenate([base, 0.6 * base + 0.8 * other, values_part], axis=1) / math.sqrt(CH)
    return result.astype(jnp.bfloat16)


def steps_of(key, dims, shards, low, top_value):
    loudness = 1.0
    for axis_at, blocks in shards:
        draws = jax.random.uniform(jax.random.fold_in(jax.random.fold_in(key, 6), axis_at), (blocks,), jnp.float32, low / len(shards), top_value / len(shards))
        loudness = loudness * jnp.repeat(jnp.exp(draws), dims[axis_at] // blocks).reshape((-1,) + (1,) * (len(dims) - 1 - axis_at))
    return loudness


def normal_values(rng, extent, spread, reach, cuts=(), held_as=jnp.bfloat16):
    values = jax.random.normal(rng, extent, jnp.float32) * spread
    if len(cuts) > 0:
        values = steps_of(rng, extent, cuts, -0.22, 0.18) * values
    return jnp.clip(values, min=-reach, max=reach).astype(held_as)


def setup_inputs(seed: int = 0) -> dict:
    seeds = jax.random.split(jax.random.key(seed), 6)
    features = draw_features(jax.random.fold_in(seeds[5], 71), 0)
    projection = draw_projection(jax.random.fold_in(seeds[5], 71), 0)
    first_kernel = normal_values(seeds[2], (3, 3, VAL, CONV), (9 * VAL) ** -0.5, 0.125)
    second_kernel = normal_values(seeds[3], (3, 3, CONV, CONV), (9 * CONV) ** -0.5, 0.1875)
    cotangent = normal_values(seeds[4], (HEIGHT, WIDTH, CONV), 1.0, 6.0, ((0, 32), (1, 8)))
    return dict(features=features, projection=projection, first_kernel=first_kernel, second_kernel=second_kernel, cotangent=cotangent)


def rounded(values):
    return lax.optimization_barrier(values.astype(jnp.bfloat16))

def as_wide(values):
    return values.astype(jnp.float32)

def pad_image(field):
    return jnp.pad(field, ((1, 1), (1, 1), (0, 0)))

def conv_apply(padded, kernel):
    rows_out = padded.shape[0] - 2
    cols_out = padded.shape[1] - 2
    result = jnp.zeros((rows_out, cols_out, kernel.shape[3]), jnp.float32)
    for tap_row in range(3):
        for tap_col in range(3):
            window = padded[tap_row:tap_row + rows_out, tap_col:tap_col + cols_out]
            result = result + jnp.einsum('rwc,cd->rwd', as_wide(window), as_wide(kernel[tap_row, tap_col]))
    return result

def conv_transpose(padded, kernel):
    rows_out = padded.shape[0] - 2
    cols_out = padded.shape[1] - 2
    result = jnp.zeros((rows_out, cols_out, kernel.shape[2]), jnp.float32)
    for tap_row in range(3):
        for tap_col in range(3):
            window = padded[2 - tap_row:2 - tap_row + rows_out, 2 - tap_col:2 - tap_col + cols_out]
            result = result + jnp.einsum('rwd,cd->rwc', as_wide(window), as_wide(kernel[tap_row, tap_col]))
    return result

def kernel_grad(padded, upstream):
    rows_out = upstream.shape[0]
    cols_out = upstream.shape[1]
    taps = []
    for tap_row in range(3):
        for tap_col in range(3):
            window = padded[tap_row:tap_row + rows_out, tap_col:tap_col + cols_out]
            taps.append(jnp.einsum('rwc,rwd->cd', as_wide(window), as_wide(upstream)))
    return jnp.stack(taps).reshape(3, 3, padded.shape[2], upstream.shape[2])

def silu_slope(pre_act):
    sigma = jax.nn.sigmoid(pre_act)
    return sigma * (1.0 + pre_act * (1.0 - sigma))

def row_forward(query_rows, key_rows, value_rows, scaling):
    query_count = query_rows.shape[0]
    block_rows = min(512, query_count)
    head_count = query_rows.shape[1]
    grouped = query_rows.reshape(query_count // block_rows, block_rows, head_count, query_rows.shape[2])

    def one_block(query_block):
        scores = scaling * jnp.einsum('qhd,khd->hqk', as_wide(query_block), as_wide(key_rows))
        maxima = lax.optimization_barrier(jnp.max(scores, axis=-1))
        exponent = jnp.exp(scores - maxima[:, :, None])
        totals = lax.optimization_barrier(jnp.sum(exponent, axis=-1))
        weighted = jnp.einsum('hqk,khd->qhd', as_wide(rounded(exponent)), as_wide(value_rows))
        return rounded(weighted / jnp.transpose(totals)[:, :, None])
    return lax.map(one_block, grouped).reshape(query_count, head_count, value_rows.shape[2])

def row_backward(query_rows, key_rows, value_rows, upstream_rows, attended_rows, scaling):
    query_count = query_rows.shape[0]
    block_rows = min(512, query_count)
    head_count = query_rows.shape[1]
    blocks_total = query_count // block_rows
    grouped_query = query_rows.reshape(blocks_total, block_rows, head_count, query_rows.shape[2])
    grouped_up = upstream_rows.reshape(blocks_total, block_rows, head_count, value_rows.shape[2])
    grouped_att = attended_rows.reshape(blocks_total, block_rows, head_count, value_rows.shape[2])

    def one_block(running, block_items):
        query_block, up_block, att_block = block_items
        scores = scaling * jnp.einsum('qhd,khd->hqk', as_wide(query_block), as_wide(key_rows))
        maxima = lax.optimization_barrier(jnp.max(scores, axis=-1))
        totals = lax.optimization_barrier(jnp.sum(jnp.exp(scores - maxima[:, :, None]), axis=-1))
        log_total = maxima + jnp.log(totals)
        soft = jnp.exp(scores - log_total[:, :, None])
        inner = jnp.transpose(lax.optimization_barrier(jnp.sum(as_wide(up_block) * as_wide(att_block), axis=-1)))
        slopes = jnp.einsum('qhd,khd->hqk', as_wide(up_block), as_wide(value_rows))
        dscore = as_wide(rounded(soft * (slopes - inner[:, :, None])))
        grad_query = scaling * jnp.einsum('hqk,khd->qhd', dscore, as_wide(key_rows))
        grad_key = running[0] + scaling * jnp.einsum('hqk,qhd->khd', dscore, as_wide(query_block))
        grad_value = running[1] + jnp.einsum('hqk,qhd->khd', as_wide(rounded(soft)), as_wide(up_block))
        return ((grad_key, grad_value), grad_query)
    zeros_pair = (jnp.zeros(key_rows.shape, jnp.float32), jnp.zeros(value_rows.shape, jnp.float32))
    sums_pair, grad_query = lax.scan(one_block, zeros_pair, (grouped_query, grouped_up, grouped_att))
    return (grad_query.reshape(query_count, head_count, query_rows.shape[2]), sums_pair[0], sums_pair[1])

def reference(features, projection, first_kernel, second_kernel, cotangent):
    head_qk = QK // HEADS
    head_val = VAL // HEADS
    scaling = head_qk ** (-0.5)
    flattened = features.reshape(HEIGHT * WIDTH, CH)
    packed = rounded(jnp.dot(flattened, projection, preferred_element_type=jnp.float32))
    query_all = packed[:, :QK].reshape(HEIGHT, WIDTH, HEADS, head_qk)
    key_all = packed[:, QK:2 * QK].reshape(HEIGHT, WIDTH, HEADS, head_qk)
    value_all = packed[:, 2 * QK:].reshape(HEIGHT, WIDTH, HEADS, head_val)

    def forward_row(row_items):
        return row_forward(row_items[0], row_items[1], row_items[2], scaling)
    attended4 = lax.map(forward_row, (query_all, key_all, value_all))
    attended = attended4.reshape(HEIGHT, WIDTH, VAL)
    attended_pad = pad_image(attended)
    pre_act = conv_apply(attended_pad, first_kernel)
    hidden = rounded(jax.nn.silu(pre_act))
    hidden_pad = pad_image(hidden)
    output_map = conv_apply(hidden_pad, second_kernel).astype(jnp.bfloat16)
    second_sum = kernel_grad(hidden_pad, cotangent)
    slope_pre = rounded(conv_transpose(pad_image(cotangent), second_kernel) * silu_slope(pre_act))
    first_sum = kernel_grad(attended_pad, slope_pre)
    upstream = rounded(conv_transpose(pad_image(slope_pre), first_kernel))
    upstream4 = upstream.reshape(HEIGHT, WIDTH, HEADS, head_val)

    def backward_row(row_items):
        return row_backward(row_items[0], row_items[1], row_items[2], row_items[3], row_items[4], scaling)
    grad_query, grad_key, grad_value = lax.map(backward_row, (query_all, key_all, value_all, upstream4, attended4))
    grad_packed = rounded(jnp.concatenate([grad_query.reshape(HEIGHT * WIDTH, QK), grad_key.reshape(HEIGHT * WIDTH, QK), grad_value.reshape(HEIGHT * WIDTH, VAL)], axis=-1))
    input_grad = jnp.dot(grad_packed, projection.T, preferred_element_type=jnp.float32).astype(jnp.bfloat16)
    projection_sum = jnp.dot(flattened.T, grad_packed, preferred_element_type=jnp.float32)
    factor = 1.0 / math.sqrt(HEIGHT * WIDTH)
    return (output_map, input_grad.reshape(HEIGHT, WIDTH, CH), projection_sum * factor, first_sum * factor, second_sum * factor)
```

```python
import math

import jax
import jax.numpy as jnp
from jax import lax
from jax.experimental import pallas as pl
from jax.experimental.pallas import tpu as pltpu
from jax.sharding import PartitionSpec as P

MESH = pl.DeviceIdType.MESH
F32 = jnp.float32
BF16 = jnp.bfloat16

QK = 128
VAL = 256
HEADS = 8


def with_halo(shard, sides, width):
    for axis, dim in sides:
        peers, length = (lax.axis_size(axis), shard.shape[dim])
        up = [(i, (i + 1) % peers) for i in range(peers - 1)]
        down = [(j, i) for i, j in up]
        last = lax.slice_in_dim(shard, length - width, length, axis=dim)
        first = lax.slice_in_dim(shard, 0, width, axis=dim)
        before = lax.ppermute(last, axis, up)
        after = lax.ppermute(first, axis, down)
        shard = jnp.concatenate([before, shard, after], axis=dim)
    return shard


def conv_apply(padded, kernel):
    rows_out = padded.shape[0] - 2
    cols_out = padded.shape[1] - 2
    result = jnp.zeros((rows_out, cols_out, kernel.shape[3]), jnp.float32)
    for tap_row in range(3):
        for tap_col in range(3):
            window = padded[tap_row : tap_row + rows_out, tap_col : tap_col + cols_out]
            result = result + jnp.einsum(
                "rwc,cd->rwd", window, kernel[tap_row, tap_col], preferred_element_type=jnp.float32
            )
    return result


def conv_transpose(padded, kernel):
    rows_out = padded.shape[0] - 2
    cols_out = padded.shape[1] - 2
    result = jnp.zeros((rows_out, cols_out, kernel.shape[2]), jnp.float32)
    for tap_row in range(3):
        for tap_col in range(3):
            window = padded[
                2 - tap_row : 2 - tap_row + rows_out, 2 - tap_col : 2 - tap_col + cols_out
            ]
            result = result + jnp.einsum(
                "rwd,cd->rwc", window, kernel[tap_row, tap_col], preferred_element_type=jnp.float32
            )
    return result


def kernel_grad(padded, upstream):
    rows_out = upstream.shape[0]
    cols_out = upstream.shape[1]
    taps = []
    for tap_row in range(3):
        for tap_col in range(3):
            window = padded[tap_row : tap_row + rows_out, tap_col : tap_col + cols_out]
            taps.append(
                jnp.einsum("rwc,rwd->cd", window, upstream, preferred_element_type=jnp.float32)
            )
    return jnp.stack(taps).reshape(3, 3, padded.shape[2], upstream.shape[2])


def silu_slope(pre_act):
    sigma = jax.nn.sigmoid(pre_act)
    return sigma * (1.0 + pre_act * (1.0 - sigma))


def row_forward(query_rows, key_rows, value_rows, scaling):
    query_count = query_rows.shape[0]
    block_rows = min(512, query_count)
    head_count = query_rows.shape[1]
    grouped = query_rows.reshape(
        query_count // block_rows, block_rows, head_count, query_rows.shape[2]
    )

    def one_block(query_block):
        scores = scaling * jnp.einsum(
            "qhd,khd->hqk", query_block, key_rows, preferred_element_type=jnp.float32
        )
        maxima = jnp.max(scores, axis=-1)
        exponent = jnp.exp(scores - maxima[:, :, None])
        totals = jnp.sum(exponent, axis=-1)
        weighted = jnp.einsum(
            "hqk,khd->qhd",
            exponent.astype(jnp.bfloat16),
            value_rows,
            preferred_element_type=jnp.float32,
        )
        return (weighted / jnp.transpose(totals)[:, :, None]).astype(jnp.bfloat16)

    return lax.map(one_block, grouped).reshape(query_count, head_count, value_rows.shape[2])


def row_backward(query_rows, key_rows, value_rows, upstream_rows, attended_rows, scaling):
    query_count = query_rows.shape[0]
    block_rows = min(512, query_count)
    head_count = query_rows.shape[1]
    blocks_total = query_count // block_rows
    grouped_query = query_rows.reshape(blocks_total, block_rows, head_count, query_rows.shape[2])
    grouped_up = upstream_rows.reshape(blocks_total, block_rows, head_count, value_rows.shape[2])
    grouped_att = attended_rows.reshape(blocks_total, block_rows, head_count, value_rows.shape[2])

    def one_block(running, block_items):
        query_block, up_block, att_block = block_items
        scores = scaling * jnp.einsum(
            "qhd,khd->hqk", query_block, key_rows, preferred_element_type=jnp.float32
        )
        maxima = jnp.max(scores, axis=-1)
        totals = jnp.sum(jnp.exp(scores - maxima[:, :, None]), axis=-1)
        log_total = maxima + jnp.log(totals)
        soft = jnp.exp(scores - log_total[:, :, None])
        inner = jnp.transpose(
            jnp.sum(up_block.astype(jnp.float32) * att_block.astype(jnp.float32), axis=-1)
        )
        slopes = jnp.einsum(
            "qhd,khd->hqk", up_block, value_rows, preferred_element_type=jnp.float32
        )
        dscore = (soft * (slopes - inner[:, :, None])).astype(jnp.bfloat16)
        grad_query = scaling * jnp.einsum(
            "hqk,khd->qhd", dscore, key_rows, preferred_element_type=jnp.float32
        )
        grad_key = running[0] + scaling * jnp.einsum(
            "hqk,qhd->khd", dscore, query_block, preferred_element_type=jnp.float32
        )
        grad_value = running[1] + jnp.einsum(
            "hqk,qhd->khd", soft.astype(jnp.bfloat16), up_block, preferred_element_type=jnp.float32
        )
        return ((grad_key, grad_value), grad_query)

    zeros_pair = (jnp.zeros(key_rows.shape, jnp.float32), jnp.zeros(value_rows.shape, jnp.float32))
    sums_pair, grad_query = lax.scan(
        one_block, zeros_pair, (grouped_query, grouped_up, grouped_att)
    )
    return (
        grad_query.reshape(query_count, head_count, query_rows.shape[2]),
        sums_pair[0],
        sums_pair[1],
    )


def remote(src, dst, send_sem, recv_sem, device):
    return pltpu.make_async_remote_copy(
        src_ref=src, dst_ref=dst, send_sem=send_sem, recv_sem=recv_sem,
        device_id=device, device_id_type=MESH,
    )


def reduce_kernel(
    first_ref, second_ref, proj_ref, w_out, p_out,
    wsend, wcore, whalf, wcol, wquarter, wrow, wfin, wgat,
    psend, pcol, pblock, prow, pfin, pcore, prgat, pmine, pgat,
    core_s, core_r, col_s, col_r, row_s, row_r,
):
    r = lax.axis_index("rows")
    c = lax.axis_index("cols")
    core = r % 2
    k = r // 2
    partner = (r + 1 - 2 * core, c)

    def col_dev(d):
        return (r, (c + d) % 8)

    def row_dev(d):
        return (2 * ((k + d) % 16) + core, c)

    def rows_at(start, size, align):
        return pl.ds(pl.multiple_of(start, align), size)

    barrier = pltpu.get_barrier_semaphore()
    pl.semaphore_signal(barrier, inc=1, device_id=partner, device_id_type=MESH)
    for d in range(1, 8):
        pl.semaphore_signal(barrier, inc=1, device_id=col_dev(d), device_id_type=MESH)
    for d in range(1, 16):
        pl.semaphore_signal(barrier, inc=1, device_id=row_dev(d), device_id_type=MESH)
    wsend[0:2304, :] = first_ref[...].astype(BF16)
    wsend[2304:3456, :] = second_ref[...].astype(BF16)
    wsend[3456:4096, :] = jnp.zeros((640, 128), BF16)
    for i in range(4):
        psend[256 * i : 256 * i + 256, :] = proj_ref[:, 128 * i : 128 * i + 128].astype(BF16)
    pl.semaphore_wait(barrier, 23)

    w1 = remote(wsend.at[rows_at(2048 * (1 - core), 2048, 2048)], wcore, core_s.at[0], core_r.at[0], partner)
    w1.start()
    p1 = []
    for d in range(1, 8):
        cp = remote(psend.at[rows_at(128 * ((c + d) % 8), 128, 128)], pcol.at[d], col_s.at[0, d], col_r.at[0, d], col_dev(d))
        cp.start()
        p1.append(cp)
    w1.wait()
    whalf[...] = (wsend[rows_at(2048 * core, 2048, 2048), :].astype(F32) + wcore[...].astype(F32)).astype(BF16)
    w2 = []
    for d in range(1, 8):
        cp = remote(whalf.at[rows_at(256 * ((c + d) % 8), 256, 256)], wcol.at[d], col_s.at[1, d], col_r.at[1, d], col_dev(d))
        cp.start()
        w2.append(cp)
    for cp in p1:
        cp.wait()
    total = psend[rows_at(128 * c, 128, 128), :].astype(F32)
    for d in range(1, 8):
        total = total + pcol[d].astype(F32)
    pblock[...] = total
    p2 = []
    for d in range(1, 16):
        cp = remote(pblock.at[rows_at(8 * ((k + d) % 16), 8, 8)], prow.at[d], row_s.at[0, d], row_r.at[0, d], row_dev(d))
        cp.start()
        p2.append(cp)
    for cp in w2:
        cp.wait()
    total = whalf[rows_at(256 * c, 256, 256), :].astype(F32)
    for d in range(1, 8):
        total = total + wcol[d].astype(F32)
    wquarter[...] = total.astype(BF16)
    w3 = []
    for d in range(1, 16):
        cp = remote(wquarter.at[rows_at(16 * ((k + d) % 16), 16, 16)], wrow.at[d], row_s.at[1, d], row_r.at[1, d], row_dev(d))
        cp.start()
        w3.append(cp)
    for cp in p2:
        cp.wait()
    total = pblock[rows_at(8 * k, 8, 8), :]
    for d in range(1, 16):
        total = total + prow[d]
    pfin[...] = total
    p3 = remote(pfin, pcore, core_s.at[1], core_r.at[1], partner)
    p3.start()
    for cp in w3:
        cp.wait()
    total = wquarter[rows_at(16 * k, 16, 16), :].astype(F32)
    for d in range(1, 16):
        total = total + wrow[d].astype(F32)
    wfin[...] = total.astype(BF16)
    mine = 2048 * core + 256 * c + 16 * k
    w4 = []
    for d in range(1, 16):
        cp = remote(wfin, wgat.at[rows_at(mine, 16, 16)], row_s.at[2, d], row_r.at[2, d], row_dev(d))
        cp.start()
        w4.append(cp)
    wgat[rows_at(mine, 16, 16), :] = wfin[...]
    p3.wait()
    pmine[...] = pfin[...] + pcore[...]
    p4 = []
    for d in range(1, 16):
        cp = remote(pmine, prgat.at[rows_at(8 * k, 8, 8)], row_s.at[3, d], row_r.at[3, d], row_dev(d))
        cp.start()
        p4.append(cp)
    prgat[rows_at(8 * k, 8, 8), :] = pmine[...]
    for cp in w4:
        cp.wait()
    w5 = []
    for d in range(1, 8):
        block = wgat.at[rows_at(2048 * core + 256 * c, 256, 256)]
        cp = remote(block, block, col_s.at[2, d], col_r.at[2, d], col_dev(d))
        cp.start()
        w5.append(cp)
    for cp in p4:
        cp.wait()
    pgat[rows_at(128 * c, 128, 128), :] = prgat[...].astype(BF16)
    p5 = []
    for d in range(1, 8):
        block = pgat.at[rows_at(128 * c, 128, 128)]
        cp = remote(block, block, col_s.at[3, d], col_r.at[3, d], col_dev(d))
        cp.start()
        p5.append(cp)
    for cp in w5:
        cp.wait()
    half = wgat.at[rows_at(2048 * core, 2048, 2048)]
    w6 = remote(half, half, core_s.at[2], core_r.at[2], partner)
    w6.start()
    for cp in p5:
        cp.wait()
    p_out[...] = pgat[...]
    w6.wait()
    w_out[...] = wgat[...]


def reduce_all(first, second, proj):
    vm = pltpu.VMEM
    dma = pltpu.SemaphoreType.DMA
    return pl.pallas_call(
        reduce_kernel,
        out_shape=(jax.ShapeDtypeStruct((4096, 128), BF16), jax.ShapeDtypeStruct((1024, 128), BF16)),
        in_specs=[pl.BlockSpec(memory_space=vm)] * 3,
        out_specs=[pl.BlockSpec(memory_space=vm)] * 2,
        scratch_shapes=[
            vm((4096, 128), BF16), vm((2048, 128), BF16), vm((2048, 128), BF16), vm((8, 256, 128), BF16),
            vm((256, 128), BF16), vm((16, 16, 128), BF16), vm((16, 128), BF16), vm((4096, 128), BF16),
            vm((1024, 128), BF16), vm((8, 128, 128), BF16), vm((128, 128), F32), vm((16, 8, 128), F32),
            vm((8, 128), F32), vm((8, 128), F32), vm((128, 128), F32), vm((8, 128), F32), vm((1024, 128), BF16),
            dma((3,)), dma((3,)), dma((4, 8)), dma((4, 8)), dma((4, 16)), dma((4, 16)),
        ],
        compiler_params=pltpu.CompilerParams(collective_id=0, has_side_effects=True),
    )(first, second, proj)


def body(features, projection, first_kernel, second_kernel, cotangent):
    height, across, channels = features.shape
    head_qk = QK // HEADS
    head_val = VAL // HEADS
    per_head = 2 * head_qk + head_val
    scaling = head_qk ** (-0.5)
    flattened = features.reshape(height * across, channels)
    packed = jnp.dot(flattened, projection, preferred_element_type=jnp.float32).astype(jnp.bfloat16)
    query_all = packed[:, :QK].reshape(height, across, HEADS, head_qk)
    key_all = packed[:, QK : 2 * QK].reshape(height, across, HEADS, head_qk)
    value_all = packed[:, 2 * QK :].reshape(height, across, HEADS, head_val)
    stacked = jnp.concatenate([query_all, key_all, value_all], axis=-1).reshape(
        height, across, HEADS * per_head
    )
    block_in = lax.all_to_all(stacked, "cols", split_axis=2, concat_axis=1, tiled=True)
    item_count, width_all, channel_count = block_in.shape
    head_local = channel_count // per_head
    split_parts = block_in.reshape(item_count, width_all, head_local, per_head)

    def one_row(row_items):
        return row_forward(row_items[0], row_items[1], row_items[2], scaling)

    result = lax.map(
        one_row,
        (
            split_parts[..., :head_qk],
            split_parts[..., head_qk : 2 * head_qk],
            split_parts[..., 2 * head_qk :],
        ),
    )
    attended_flat = lax.all_to_all(
        result.reshape(item_count, width_all, head_local * head_val),
        "cols",
        split_axis=1,
        concat_axis=2,
        tiled=True,
    )
    attended4 = attended_flat.reshape(height, across, HEADS, head_val)
    attended = attended4.reshape(height, across, VAL)
    attended_pad = with_halo(attended, (("rows", 0), ("cols", 1)), 1)
    pre_act = conv_apply(attended_pad, first_kernel)
    hidden = jax.nn.silu(pre_act).astype(jnp.bfloat16)
    hidden_pad = with_halo(hidden, (("rows", 0), ("cols", 1)), 1)
    output_map = conv_apply(hidden_pad, second_kernel).astype(jnp.bfloat16)
    cotangent_pad = with_halo(cotangent, (("rows", 0), ("cols", 1)), 1)
    second_sum = kernel_grad(hidden_pad, cotangent)
    slope_pre = (conv_transpose(cotangent_pad, second_kernel) * silu_slope(pre_act)).astype(
        jnp.bfloat16
    )
    slope_pad = with_halo(slope_pre, (("rows", 0), ("cols", 1)), 1)
    first_sum = kernel_grad(attended_pad, slope_pre)
    upstream = conv_transpose(slope_pad, first_kernel).astype(jnp.bfloat16)
    stacked_part = lax.all_to_all(stacked, "cols", split_axis=2, concat_axis=1, tiled=True)
    upstream_part = lax.all_to_all(upstream, "cols", split_axis=2, concat_axis=1, tiled=True)
    attended_part = lax.all_to_all(attended, "cols", split_axis=2, concat_axis=1, tiled=True)
    item_count, width_all, channel_count = stacked_part.shape
    head_local = channel_count // per_head
    split_parts = stacked_part.reshape(item_count, width_all, head_local, per_head)
    up_parts = upstream_part.reshape(item_count, width_all, head_local, head_val)
    att_parts = attended_part.reshape(item_count, width_all, head_local, head_val)

    def one_row(row_items):
        return row_backward(
            row_items[0], row_items[1], row_items[2], row_items[3], row_items[4], scaling
        )

    grads = lax.map(
        one_row,
        (
            split_parts[..., :head_qk],
            split_parts[..., head_qk : 2 * head_qk],
            split_parts[..., 2 * head_qk :],
            up_parts,
            att_parts,
        ),
    )
    joined = (
        jnp.concatenate(grads, axis=-1)
        .astype(jnp.bfloat16)
        .reshape(item_count, width_all, head_local * per_head)
    )
    grad_heads = lax.all_to_all(joined, "cols", split_axis=1, concat_axis=2, tiled=True)
    grad_split = grad_heads.reshape(height * across, HEADS, per_head)
    grad_packed = jnp.concatenate(
        [
            grad_split[:, :, :head_qk].reshape(height * across, QK),
            grad_split[:, :, head_qk : 2 * head_qk].reshape(height * across, QK),
            grad_split[:, :, 2 * head_qk :].reshape(height * across, VAL),
        ],
        axis=-1,
    )
    input_grad = jnp.dot(grad_packed, projection.T, preferred_element_type=jnp.float32).astype(
        jnp.bfloat16
    )
    projection_sum = jnp.einsum(
        "pc,pd->cd", flattened, grad_packed, preferred_element_type=jnp.float32
    )
    w_all, p_all = reduce_all(first_sum.reshape(2304, 128), second_sum.reshape(1152, 128), projection_sum)
    pixel_count = height * across * lax.axis_size("rows") * lax.axis_size("cols")
    factor = 1.0 / math.sqrt(pixel_count)
    w_all = w_all.astype(F32) * factor
    p_all = p_all.astype(F32) * factor
    return (
        output_map,
        input_grad.reshape(height, across, channels),
        p_all.reshape(4, 256, 128).transpose(1, 0, 2).reshape(256, 512),
        w_all[:2304].reshape(3, 3, 256, 128),
        w_all[2304:3456].reshape(3, 3, 128, 128),
    )


def solution(mesh):
    placed = (P("rows", "cols", None), P(), P(), P(), P("rows", "cols", None))
    return jax.shard_map(
        body,
        mesh=mesh,
        in_specs=placed,
        out_specs=(P("rows", "cols", None), P("rows", "cols", None), P(), P(), P()),
        check_vma=False,
    )
```

```python
import math

import jax
import jax.numpy as jnp
from jax import lax
from jax.experimental import pallas as pl
from jax.experimental.pallas import tpu as pltpu
from jax.sharding import PartitionSpec as P

MESH = pl.DeviceIdType.MESH
F32 = jnp.float32
BF16 = jnp.bfloat16
HEIGHT = 32
WIDTH = 1024


def remote(src, dst, send_sem, recv_sem, device):
    return pltpu.make_async_remote_copy(
        src_ref=src, dst_ref=dst, send_sem=send_sem, recv_sem=recv_sem,
        device_id=device, device_id_type=MESH,
    )


def at(start, size, align):
    return pl.ds(pl.multiple_of(start, align), size)


def dot(a, b):
    return jnp.dot(a, b, preferred_element_type=F32)


def dot_nt(a, b):
    return lax.dot_general(a, b, (((1,), (1,)), ((), ())), preferred_element_type=F32)


def dot_tn(a, b):
    return lax.dot_general(a, b, (((0,), (0,)), ((), ())), preferred_element_type=F32)


def shifted(x):
    return pltpu.roll(x, 1, 0), x, pltpu.roll(x, 143, 0)


def wait_all(copies):
    for cp in copies:
        cp.wait()


def block_kernel(
    feat, proj, k1, k2, cot, out_ref, ig_ref, w_out, p_out,
    qkv_send, qkv, att_t, inv_ref, s_ref, e_ref, d_ref, kmat, vext, vext_t,
    att_send, att_recv, attx, imc, cot_l, cot_r, cotx, cim, k2t, k1t, tc,
    hx, sx, up_send, up_t, u_ext, g_t, g_recv, featx,
    wsend, wcore, whalf, wcol, wquarter, wrow, wfin, wgat,
    pblock, prow, pfin, pcore, prgat, pmine, pgat, pall,
    core_s, core_r, col_s, col_r, row_s, row_r, halo_s, halo_r,
):
    r = lax.axis_index("rows")
    c = lax.axis_index("cols")
    core = r % 2
    k = r // 2
    partner = (r + 1 - 2 * core, c)

    def col_dev(d):
        return (r, (c + d) % 8)

    def row_dev(d):
        return (2 * ((k + d) % 16) + core, c)

    def near(d):
        return ((r + d + 32) % 32, c)

    def to_cols(kind, src_of, dst):
        copies = []
        for d in range(1, 8):
            cp = remote(src_of((c + d) % 8), dst(d), col_s.at[kind, d], col_r.at[kind, d], col_dev(d))
            cp.start()
            copies.append(cp)
        return copies

    def to_rows(kind, src_of, dst):
        copies = []
        for d in range(1, 16):
            cp = remote(src_of((k + d) % 16), dst(d), row_s.at[kind, d], row_r.at[kind, d], row_dev(d))
            cp.start()
            copies.append(cp)
        return copies

    def to_near(kind, src, slots):
        copies = []
        for n, d in enumerate((-2, -1, 1, 2)):
            cp = remote(src, slots.at[2 - d], halo_s.at[kind, n], halo_r.at[kind, n], near(d))
            cp.start()
            copies.append(cp)
        return copies

    barrier = pltpu.get_barrier_semaphore()
    pl.semaphore_signal(barrier, inc=1, device_id=partner, device_id_type=MESH)
    pl.semaphore_signal(barrier, inc=1, device_id=near(2 * core - 1), device_id_type=MESH)
    for d in range(1, 8):
        pl.semaphore_signal(barrier, inc=1, device_id=col_dev(d), device_id_type=MESH)
    for d in range(1, 16):
        pl.semaphore_signal(barrier, inc=1, device_id=row_dev(d), device_id_type=MESH)

    packed = jnp.transpose(dot(feat[...], proj[...])).astype(BF16)
    for h in range(8):
        qkv_send[64 * h : 64 * h + 16, :] = packed[16 * h : 16 * h + 16]
        qkv_send[64 * h + 16 : 64 * h + 32, :] = packed[128 + 16 * h : 144 + 16 * h]
        qkv_send[64 * h + 32 : 64 * h + 64, :] = packed[256 + 32 * h : 288 + 32 * h]
    pl.semaphore_wait(barrier, 24)
    my_lanes = at(128 * c, 128, 128)
    qkv_copies = to_cols(
        0, lambda j: qkv_send.at[at(64 * j, 64, 64), :], lambda d: qkv.at[:, my_lanes]
    )
    left = remote(cot.at[112:128], cot_l, halo_s.at[2, 0], halo_r.at[2, 0], col_dev(1))
    left.start()
    right = remote(cot.at[0:16], cot_r, halo_s.at[2, 1], halo_r.at[2, 1], col_dev(7))
    right.start()
    qkv[:, my_lanes] = qkv_send[at(64 * c, 64, 64), :]
    for a in range(3):
        for b in range(3):
            n = 3 * a + b
            k2t[a, 128 * b : 128 * b + 128, :] = jnp.transpose(
                k2[128 * n : 128 * n + 128, :].astype(F32)
            ).astype(BF16)
            k1t[a, 128 * b : 128 * b + 128, :] = jnp.transpose(
                k1[256 * n : 256 * n + 256, :].astype(F32)
            ).astype(BF16)
    index = lax.broadcasted_iota(jnp.int32, (144, 128), 0)
    low_end = 136 - 8 * (c // 7)
    high_start = 136 + 8 * ((7 - c) // 7)

    def in_image(row):
        return jnp.where((row >= 0) & (row < HEIGHT), 1, 0)

    left.wait()
    right.wait()
    cotx[2] = jnp.where(
        (index < low_end) | (index >= high_start),
        jnp.concatenate([cot[...].astype(F32), cot_r[0:8, :].astype(F32), cot_l[8:16, :].astype(F32)]),
        0.0,
    ).astype(BF16)
    cot_copies = to_near(0, cotx.at[2], cotx)
    wait_all(qkv_copies)
    feat_copies = to_cols(1, lambda j: feat, lambda d: featx.at[at(128 * c, 128, 128), :])
    featx[at(128 * c, 128, 128), :] = feat[...]

    kmat[...] = (jnp.transpose(qkv[16:32, :].astype(F32)) * 0.25).astype(BF16)
    vext_t[0:32, :] = qkv[32:64, :]
    extra = lax.broadcasted_iota(jnp.int32, (16, 1024), 0)
    vext_t[32:48, :] = jnp.where(extra < 2, 1.0, 0.0).astype(BF16)
    vext[...] = jnp.transpose(vext_t[...].astype(F32)).astype(BF16)
    for ib in range(4):
        lanes = slice(256 * ib, 256 * ib + 256)
        q_block = qkv[0:16, lanes]
        top = None
        for jc in range(8):
            s = dot(kmat[128 * jc : 128 * jc + 128, :], q_block)
            s_ref[ib % 2, 128 * jc : 128 * jc + 128, :] = s
            part = jnp.max(s.reshape(16, 8, 256), axis=0)
            top = part if top is None else jnp.maximum(top, part)
        top = jnp.max(top, axis=0, keepdims=True)
        for jc in range(8):
            rows = slice(128 * jc, 128 * jc + 128)
            e_ref[rows, lanes] = jnp.exp(s_ref[ib % 2, rows, :] - top).astype(BF16)
        weighted = dot(vext_t[...], e_ref[:, lanes])
        inverse = 1.0 / weighted[32:33, :]
        inv_ref[0:1, lanes] = inverse
        att_t[:, lanes] = (weighted[0:32, :] * inverse).astype(BF16)

    lane = lax.broadcasted_iota(jnp.int32, (32, 128), 1)
    zero = jnp.zeros((32, 128), F32)
    for j in range(8):
        after = att_t[:, 128 * j + 128 : 128 * j + 256].astype(F32) if j < 7 else zero
        before = att_t[:, 128 * j - 128 : 128 * j].astype(F32) if j > 0 else zero
        att_send[j, :, 0:128] = att_t[:, 128 * j : 128 * j + 128]
        att_send[j, :, 128:256] = jnp.where(lane < 64, after, before).astype(BF16)
    att_copies = to_cols(2, lambda j: att_send.at[j], lambda d: att_recv.at[at(32 * c, 32, 32), :])
    att_recv[at(32 * c, 32, 32), :] = att_send[c]

    wait_all(cot_copies)
    for slot in range(5):
        x = cotx[slot].astype(F32) * in_image(r - 2 + slot).astype(F32)
        low, mid, high = shifted(x)
        cim[slot, :, 0:128] = high.astype(BF16)
        cim[slot, :, 128:256] = mid.astype(BF16)
        cim[slot, :, 256:384] = low.astype(BF16)
    for t in range(3):
        tc[t] = (
            dot(cim[t + 2], k2t[0]) + dot(cim[t + 1], k2t[1]) + dot(cim[t], k2t[2])
        )

    wait_all(att_copies)
    turned = jnp.transpose(att_recv[...].astype(F32))
    attx[2] = jnp.concatenate([turned[0:136], turned[248:256]]).astype(BF16)
    near_copies = to_near(1, attx.at[2], attx)

    def columns(slot):
        x = attx[slot].astype(F32) * in_image(r - 2 + slot).astype(F32)
        low, mid, high = shifted(x)
        imc[slot, :, 0:256] = low.astype(BF16)
        imc[slot, :, 256:512] = mid.astype(BF16)
        imc[slot, :, 512:768] = high.astype(BF16)

    columns(2)
    wait_all(near_copies)
    for slot in (0, 1, 3, 4):
        columns(slot)

    for t in range(3):
        pre = (
            dot(imc[t], k1[0:768, :])
            + dot(imc[t + 1], k1[768:1536, :])
            + dot(imc[t + 2], k1[1536:2304, :])
        )
        valid = in_image(r - 1 + t)
        keep = (index < low_end * valid) | (index >= 144 - (144 - high_start) * valid)
        sigma = 1.0 / (1.0 + jnp.exp(-pre))
        slope = jnp.where(keep, tc[t] * (sigma * (1.0 + pre * (1.0 - sigma))), 0.0)
        low, mid, high = shifted(slope)
        sx[t, :, 0:128] = high.astype(BF16)
        sx[t, :, 128:256] = mid.astype(BF16)
        sx[t, :, 256:384] = low.astype(BF16)
        hidden = jnp.where(keep, pre * sigma, 0.0)
        low, mid, high = shifted(hidden)
        hx[t, :, 0:128] = low.astype(BF16)
        hx[t, :, 128:256] = mid.astype(BF16)
        hx[t, :, 256:384] = high.astype(BF16)

    upstream = (
        dot(sx[2, 0:128, :], k1t[0]) + dot(sx[1, 0:128, :], k1t[1]) + dot(sx[0, 0:128, :], k1t[2])
    )
    up_send[...] = jnp.transpose(upstream).astype(BF16)
    up_copies = to_cols(3, lambda j: up_send.at[at(32 * j, 32, 32), :], lambda d: up_t.at[:, my_lanes])
    up_t[:, my_lanes] = up_send[at(32 * c, 32, 32), :]

    slope_own = sx[1, 0:128, 128:256]
    for a in range(3):
        wsend[768 * a : 768 * a + 768, :] = dot_tn(imc[a + 1, 0:128, :], slope_own).astype(BF16)
        wsend[2304 + 384 * a : 2688 + 384 * a, :] = dot_tn(hx[a, 0:128, :], cot[...]).astype(BF16)
    wsend[3456:4096, :] = jnp.zeros((640, 128), BF16)
    w1 = remote(wsend.at[at(2048 * (1 - core), 2048, 2048)], wcore, core_s.at[0], core_r.at[0], partner)
    w1.start()
    out_ref[...] = (
        dot(hx[0, 0:128, :], k2[0:384, :])
        + dot(hx[1, 0:128, :], k2[384:768, :])
        + dot(hx[2, 0:128, :], k2[768:1152, :])
    ).astype(BF16)

    wait_all(up_copies)
    scaled = (up_t[...].astype(F32) * inv_ref[0:1, :]).astype(BF16)
    u_ext[0:32, :] = scaled
    inner = jnp.sum(scaled.astype(F32) * att_t[...].astype(F32), axis=0, keepdims=True)
    inner_high = inner.astype(BF16).astype(F32)
    extra = lax.broadcasted_iota(jnp.int32, (16, 1024), 0)
    u_ext[32:48, :] = jnp.where(
        extra == 0, -inner_high, jnp.where(extra == 1, inner_high - inner, 0.0)
    ).astype(BF16)

    def backward(ib):
        lanes = slice(256 * ib, 256 * ib + 256)
        u_block = u_ext[:, lanes]
        for jc in range(8):
            rows = slice(128 * jc, 128 * jc + 128)
            slopes = dot(vext[rows, :], u_block)
            d_ref[rows, lanes] = (e_ref[rows, lanes].astype(F32) * slopes).astype(BF16)
        g_t[0:16, lanes] = (dot(qkv[16:32, :], d_ref[:, lanes]) * 0.25).astype(BF16)

    backward(0)
    backward(1)
    w1.wait()
    for n in range(8):
        rows = slice(256 * n, 256 * n + 256)
        mine = wsend[at(2048 * core + 256 * n, 256, 256), :]
        whalf[rows, :] = (mine.astype(F32) + wcore[rows, :].astype(F32)).astype(BF16)
    w2 = to_cols(4, lambda j: whalf.at[at(256 * j, 256, 256), :], lambda d: wcol.at[d])
    backward(2)
    backward(3)
    g_t[32:64, :] = dot_nt(u_ext[0:32, :], e_ref[...]).astype(BF16)
    g_t[16:32, :] = (dot_nt(qkv[0:16, :], d_ref[...]) * 0.25).astype(BF16)
    g_copies = to_cols(5, lambda j: g_t.at[:, at(128 * j, 128, 128)], lambda d: g_recv.at[at(64 * c, 64, 64), :])
    g_recv[at(64 * c, 64, 64), :] = g_t[:, my_lanes]

    wait_all(feat_copies)
    turned = dot(g_t[...], featx[...])
    pblock[0:64, :] = turned[:, 0:128]
    pblock[64:128, :] = turned[:, 128:256]
    p2 = to_rows(0, lambda j: pblock.at[at(8 * j, 8, 8), :], lambda d: prow.at[d])

    wait_all(w2)
    total = whalf[at(256 * c, 256, 256), :].astype(F32)
    for d in range(1, 8):
        total = total + wcol[d].astype(F32)
    wquarter[...] = total.astype(BF16)
    w3 = to_rows(1, lambda j: wquarter.at[at(16 * j, 16, 16), :], lambda d: wrow.at[d])

    wait_all(g_copies)
    parts = []
    for first, size in ((0, 16), (16, 16), (32, 32)):
        for h in range(8):
            parts.append(g_recv[64 * h + first : 64 * h + first + size, :].astype(F32))
    grads = jnp.transpose(jnp.concatenate(parts)).astype(BF16)
    ig_ref[...] = dot_nt(grads, proj[...]).astype(BF16)

    wait_all(p2)
    total = pblock[at(8 * k, 8, 8), :]
    for d in range(1, 16):
        total = total + prow[d]
    pfin[...] = total
    p3 = remote(pfin, pcore, core_s.at[1], core_r.at[1], partner)
    p3.start()
    wait_all(w3)
    total = wquarter[at(16 * k, 16, 16), :].astype(F32)
    for d in range(1, 16):
        total = total + wrow[d].astype(F32)
    wfin[...] = total.astype(BF16)
    mine = 2048 * core + 256 * c + 16 * k
    w4 = to_rows(2, lambda j: wfin, lambda d: wgat.at[at(mine, 16, 16), :])
    wgat[at(mine, 16, 16), :] = wfin[...]
    p3.wait()
    pmine[...] = pfin[...] + pcore[...]
    p4 = to_rows(3, lambda j: pmine, lambda d: prgat.at[at(8 * k, 8, 8), :])
    prgat[at(8 * k, 8, 8), :] = pmine[...]
    wait_all(w4)
    mine = wgat.at[at(2048 * core + 256 * c, 256, 256), :]
    w5 = to_cols(6, lambda j: mine, lambda d: mine)
    wait_all(p4)
    pgat[at(128 * c, 128, 128), :] = prgat[...].astype(BF16)
    block = pgat.at[at(128 * c, 128, 128), :]
    p5 = to_cols(7, lambda j: block, lambda d: block)
    wait_all(w5)
    half = wgat.at[at(2048 * core, 2048, 2048), :]
    w6 = remote(half, half, core_s.at[2], core_r.at[2], partner)
    w6.start()
    wait_all(p5)
    for h in range(8):
        for side in range(2):
            base = 128 * h + 64 * side
            lanes = slice(128 * side, 128 * side + 128)
            pall[16 * h : 16 * h + 16, lanes] = pgat[base : base + 16, :]
            pall[128 + 16 * h : 144 + 16 * h, lanes] = pgat[base + 16 : base + 32, :]
            pall[256 + 32 * h : 288 + 32 * h, lanes] = pgat[base + 32 : base + 64, :]
    p_out[...] = jnp.transpose(pall[...].astype(F32)) * (1.0 / math.sqrt(HEIGHT * WIDTH))
    w6.wait()
    w_out[...] = wgat[...]


def body(features, projection, first_kernel, second_kernel, cotangent):
    vm = pltpu.VMEM
    dma = pltpu.SemaphoreType.DMA
    out, grad, weights, proj_grad = pl.pallas_call(
        block_kernel,
        out_shape=(
            jax.ShapeDtypeStruct((128, 128), BF16),
            jax.ShapeDtypeStruct((128, 256), BF16),
            jax.ShapeDtypeStruct((4096, 128), BF16),
            jax.ShapeDtypeStruct((256, 512), F32),
        ),
        in_specs=[pl.BlockSpec(memory_space=vm)] * 5,
        out_specs=[pl.BlockSpec(memory_space=vm)] * 4,
        scratch_shapes=[
            vm((512, 128), BF16), vm((64, 1024), BF16), vm((32, 1024), BF16), vm((8, 1024), F32),
            vm((2, 1024, 256), F32), vm((1024, 1024), BF16), vm((1024, 1024), BF16),
            vm((1024, 16), BF16), vm((1024, 48), BF16), vm((48, 1024), BF16),
            vm((8, 32, 256), BF16), vm((256, 256), BF16), vm((5, 144, 256), BF16), vm((5, 144, 768), BF16),
            vm((16, 128), BF16), vm((16, 128), BF16), vm((5, 144, 128), BF16), vm((5, 144, 384), BF16),
            vm((3, 384, 128), BF16), vm((3, 384, 256), BF16), vm((3, 144, 128), F32),
            vm((3, 144, 384), BF16), vm((3, 144, 384), BF16),
            vm((256, 128), BF16), vm((32, 1024), BF16), vm((48, 1024), BF16),
            vm((64, 1024), BF16), vm((512, 128), BF16), vm((1024, 256), BF16),
            vm((4096, 128), BF16), vm((2048, 128), BF16), vm((2048, 128), BF16), vm((8, 256, 128), BF16),
            vm((256, 128), BF16), vm((16, 16, 128), BF16), vm((16, 128), BF16), vm((4096, 128), BF16),
            vm((128, 128), F32), vm((16, 8, 128), F32), vm((8, 128), F32), vm((8, 128), F32),
            vm((128, 128), F32), vm((8, 128), F32), vm((1024, 128), BF16), vm((512, 256), BF16),
            dma((3,)), dma((3,)), dma((8, 8)), dma((8, 8)), dma((4, 16)), dma((4, 16)), dma((3, 4)), dma((3, 4)),
        ],
        compiler_params=pltpu.CompilerParams(collective_id=0, has_side_effects=True),
    )(
        features.reshape(128, 256),
        projection,
        first_kernel.reshape(2304, 128),
        second_kernel.reshape(1152, 128),
        cotangent.reshape(128, 128),
    )
    factor = 1.0 / math.sqrt(HEIGHT * WIDTH)
    return (
        out.reshape(1, 128, 128),
        grad.reshape(1, 128, 256),
        proj_grad,
        (weights[:2304].astype(F32) * factor).reshape(3, 3, 256, 128),
        (weights[2304:3456].astype(F32) * factor).reshape(3, 3, 128, 128),
    )


def solution(mesh):
    placed = (P("rows", "cols", None), P(), P(), P(), P("rows", "cols", None))
    return jax.shard_map(
        body,
        mesh=mesh,
        in_specs=placed,
        out_specs=(P("rows", "cols", None), P("rows", "cols", None), P(), P(), P()),
        check_vma=False,
    )
```

```python
import math

import jax
import jax.numpy as jnp
from jax import lax
from jax.experimental import pallas as pl
from jax.experimental.pallas import tpu as pltpu
from jax.sharding import PartitionSpec as P

MESH = pl.DeviceIdType.MESH
F32 = jnp.float32
BF16 = jnp.bfloat16
HEIGHT = 32
WIDTH = 1024


def remote(src, dst, send_sem, recv_sem, device):
    return pltpu.make_async_remote_copy(
        src_ref=src, dst_ref=dst, send_sem=send_sem, recv_sem=recv_sem,
        device_id=device, device_id_type=MESH,
    )


def at(start, size, align):
    return pl.ds(pl.multiple_of(start, align), size)


def dot(a, b):
    return jnp.dot(a, b, preferred_element_type=F32)


def dot_nt(a, b):
    return lax.dot_general(a, b, (((1,), (1,)), ((), ())), preferred_element_type=F32)


def dot_tn(a, b):
    return lax.dot_general(a, b, (((0,), (0,)), ((), ())), preferred_element_type=F32)


def shifted(x):
    return pltpu.roll(x, 1, 0), x, pltpu.roll(x, 143, 0)


def wait_all(copies):
    for cp in copies:
        cp.wait()


def block_kernel(
    feat_in, proj_in, k1_in, k2_in, cot_in, out_ref, ig_ref, w_out, p_out,
    feat, proj, k1, k2, cot,
    qkv_send, qkv, att_t, inv_ref, s_ref, e_ref, d_ref, kmat, vext, vext_t,
    att_send, att_recv, attx, imc, cot_l, cot_r, cotx, cim, k2t, k1t, tc,
    hx, sx, up_send, up_t, u_ext, g_t, g_recv, featx,
    wsend, wcore, whalf, wcol, wquarter, wrow, wfin, wrgat, wgat,
    pblock, prow, pfin, pcore, prgat, pmine, pgat,
    core_s, core_r, col_s, col_r, row_s, row_r, halo_s, halo_r, load_s,
):
    r = lax.axis_index("rows")
    c = lax.axis_index("cols")
    core = r % 2
    k = r // 2
    partner = (r + 1 - 2 * core, c)

    def col_dev(d):
        return (r, (c + d) % 8)

    def row_dev(d):
        return (2 * ((k + d) % 16) + core, c)

    def near(d):
        return ((r + d + 32) % 32, c)

    def to_cols(kind, src_of, dst):
        copies = []
        for d in range(1, 8):
            cp = remote(src_of((c + d) % 8), dst(d), col_s.at[kind, d], col_r.at[kind, d], col_dev(d))
            cp.start()
            copies.append(cp)
        return copies

    def to_rows(kind, src_of, dst):
        copies = []
        for d in range(1, 16):
            cp = remote(src_of((k + d) % 16), dst(d), row_s.at[kind, d], row_r.at[kind, d], row_dev(d))
            cp.start()
            copies.append(cp)
        return copies

    def to_near(kind, src, slots):
        copies = []
        for n, d in enumerate((-2, -1, 1, 2)):
            cp = remote(src, slots.at[2 - d], halo_s.at[kind, n], halo_r.at[kind, n], near(d))
            cp.start()
            copies.append(cp)
        return copies

    barrier = pltpu.get_barrier_semaphore()
    pl.semaphore_signal(barrier, inc=1, device_id=partner, device_id_type=MESH)
    pl.semaphore_signal(barrier, inc=1, device_id=near(2 * core - 1), device_id_type=MESH)
    for d in range(1, 8):
        pl.semaphore_signal(barrier, inc=1, device_id=col_dev(d), device_id_type=MESH)
    for d in range(1, 16):
        pl.semaphore_signal(barrier, inc=1, device_id=row_dev(d), device_id_type=MESH)

    loads = []
    for n, (src, dst) in enumerate(
        ((feat_in, feat), (proj_in, proj), (cot_in, cot), (k2_in, k2), (k1_in, k1))
    ):
        cp = pltpu.make_async_copy(src, dst, load_s.at[n])
        cp.start()
        loads.append(cp)

    wait_all(loads[0:2])
    packed = jnp.transpose(dot(feat[...], proj[...])).astype(BF16)
    for h in range(8):
        qkv_send[64 * h : 64 * h + 16, :] = packed[16 * h : 16 * h + 16]
        qkv_send[64 * h + 16 : 64 * h + 32, :] = packed[128 + 16 * h : 144 + 16 * h]
        qkv_send[64 * h + 32 : 64 * h + 64, :] = packed[256 + 32 * h : 288 + 32 * h]
    wait_all(loads[2:5])
    pl.semaphore_wait(barrier, 24)
    my_lanes = at(128 * c, 128, 128)
    qkv_copies = to_cols(
        0, lambda j: qkv_send.at[at(64 * j, 64, 64), :], lambda d: qkv.at[:, my_lanes]
    )
    left = remote(cot.at[112:128], cot_l, halo_s.at[2, 0], halo_r.at[2, 0], col_dev(1))
    left.start()
    right = remote(cot.at[0:16], cot_r, halo_s.at[2, 1], halo_r.at[2, 1], col_dev(7))
    right.start()
    qkv[:, my_lanes] = qkv_send[at(64 * c, 64, 64), :]
    for a in range(3):
        for b in range(3):
            n = 3 * a + b
            k2t[a, 128 * b : 128 * b + 128, :] = jnp.transpose(
                k2[128 * n : 128 * n + 128, :].astype(F32)
            ).astype(BF16)
            k1t[a, 128 * b : 128 * b + 128, :] = jnp.transpose(
                k1[256 * n : 256 * n + 256, :].astype(F32)
            ).astype(BF16)
    index = lax.broadcasted_iota(jnp.int32, (144, 128), 0)
    low_end = 136 - 8 * (c // 7)
    high_start = 136 + 8 * ((7 - c) // 7)

    def in_image(row):
        return jnp.where((row >= 0) & (row < HEIGHT), 1, 0)

    left.wait()
    right.wait()
    cotx[2] = jnp.where(
        (index < low_end) | (index >= high_start),
        jnp.concatenate([cot[...].astype(F32), cot_r[0:8, :].astype(F32), cot_l[8:16, :].astype(F32)]),
        0.0,
    ).astype(BF16)
    cot_copies = to_near(0, cotx.at[2], cotx)
    wait_all(qkv_copies)

    kmat[...] = (jnp.transpose(qkv[16:32, :].astype(F32)) * 0.25).astype(BF16)
    vext_t[0:32, :] = qkv[32:64, :]
    extra = lax.broadcasted_iota(jnp.int32, (16, 1024), 0)
    vext_t[32:48, :] = jnp.where(extra < 2, 1.0, 0.0).astype(BF16)
    vext[...] = jnp.transpose(vext_t[...].astype(F32)).astype(BF16)
    lane = lax.broadcasted_iota(jnp.int32, (32, 128), 1)
    zero = jnp.zeros((32, 128), F32)

    def send_attended(j):
        after = att_t[:, 128 * j + 128 : 128 * j + 256].astype(F32) if j < 7 else zero
        before = att_t[:, 128 * j - 128 : 128 * j].astype(F32) if j > 0 else zero
        att_send[j, :, 0:128] = att_t[:, 128 * j : 128 * j + 128]
        att_send[j, :, 128:256] = jnp.where(lane < 64, after, before).astype(BF16)

        @pl.when(c != j)
        def _():
            d = (j - c + 8) % 8
            remote(
                att_send.at[j], att_recv.at[at(32 * c, 32, 32), :], col_s.at[2, d], col_r.at[2, d], (r, j)
            ).start()

    for ib in range(4):
        lanes = slice(256 * ib, 256 * ib + 256)
        q_block = qkv[0:16, lanes]
        top = None
        for jc in range(8):
            s = dot(kmat[128 * jc : 128 * jc + 128, :], q_block)
            s_ref[ib % 2, 128 * jc : 128 * jc + 128, :] = s
            part = jnp.max(s.reshape(16, 8, 256), axis=0)
            top = part if top is None else jnp.maximum(top, part)
        top = jnp.max(top, axis=0, keepdims=True)
        for jc in range(8):
            rows = slice(128 * jc, 128 * jc + 128)
            e_ref[rows, lanes] = jnp.exp(s_ref[ib % 2, rows, :] - top).astype(BF16)
        weighted = dot(vext_t[...], e_ref[:, lanes])
        inverse = 1.0 / weighted[32:33, :]
        inv_ref[0:1, lanes] = inverse
        att_t[:, lanes] = (weighted[0:32, :] * inverse).astype(BF16)
        for j in ((0,), (1, 2), (3, 4), (5, 6, 7))[ib]:
            send_attended(j)

    feat_copies = to_cols(1, lambda j: feat, lambda d: featx.at[at(128 * c, 128, 128), :])
    featx[at(128 * c, 128, 128), :] = feat[...]
    att_recv[at(32 * c, 32, 32), :] = att_send[c]

    wait_all(cot_copies)
    for slot in range(5):
        x = cotx[slot].astype(F32) * in_image(r - 2 + slot).astype(F32)
        low, mid, high = shifted(x)
        cim[slot, :, 0:128] = high.astype(BF16)
        cim[slot, :, 128:256] = mid.astype(BF16)
        cim[slot, :, 256:384] = low.astype(BF16)
    for t in range(3):
        tc[t] = (
            dot(cim[t + 2], k2t[0]) + dot(cim[t + 1], k2t[1]) + dot(cim[t], k2t[2])
        )

    for d in range(1, 8):
        remote(
            att_send.at[(c + d) % 8], att_recv.at[at(32 * c, 32, 32), :],
            col_s.at[2, d], col_r.at[2, d], col_dev(d),
        ).wait()
    turned = jnp.transpose(att_recv[...].astype(F32))
    attx[2] = jnp.concatenate([turned[0:136], turned[248:256]]).astype(BF16)
    near_copies = to_near(1, attx.at[2], attx)

    def columns(slot):
        x = attx[slot].astype(F32) * in_image(r - 2 + slot).astype(F32)
        low, mid, high = shifted(x)
        imc[slot, :, 0:256] = low.astype(BF16)
        imc[slot, :, 256:512] = mid.astype(BF16)
        imc[slot, :, 512:768] = high.astype(BF16)

    columns(2)
    wait_all(near_copies)
    for slot in (0, 1, 3, 4):
        columns(slot)

    for t in range(3):
        pre = (
            dot(imc[t], k1[0:768, :])
            + dot(imc[t + 1], k1[768:1536, :])
            + dot(imc[t + 2], k1[1536:2304, :])
        )
        valid = in_image(r - 1 + t)
        keep = (index < low_end * valid) | (index >= 144 - (144 - high_start) * valid)
        sigma = 1.0 / (1.0 + jnp.exp(-pre))
        slope = jnp.where(keep, tc[t] * (sigma * (1.0 + pre * (1.0 - sigma))), 0.0)
        low, mid, high = shifted(slope)
        sx[t, :, 0:128] = high.astype(BF16)
        sx[t, :, 128:256] = mid.astype(BF16)
        sx[t, :, 256:384] = low.astype(BF16)
        hidden = jnp.where(keep, pre * sigma, 0.0)
        low, mid, high = shifted(hidden)
        hx[t, :, 0:128] = low.astype(BF16)
        hx[t, :, 128:256] = mid.astype(BF16)
        hx[t, :, 256:384] = high.astype(BF16)

    upstream = (
        dot(sx[2, 0:128, :], k1t[0]) + dot(sx[1, 0:128, :], k1t[1]) + dot(sx[0, 0:128, :], k1t[2])
    )
    up_send[...] = jnp.transpose(upstream).astype(BF16)
    up_copies = to_cols(3, lambda j: up_send.at[at(32 * j, 32, 32), :], lambda d: up_t.at[:, my_lanes])
    up_t[:, my_lanes] = up_send[at(32 * c, 32, 32), :]

    def w_core(n):
        cp = remote(
            wsend.at[at(2048 * n + 1024 * (1 - core), 1024, 1024)], wcore.at[n], core_s.at[n], core_r.at[n], partner
        )
        cp.start()
        return cp

    def w_cols(n, copy):
        copy.wait()
        for m in range(4):
            rows = slice(256 * m, 256 * m + 256)
            mine = wsend[at(2048 * n + 1024 * core + 256 * m, 256, 256), :]
            whalf[n, rows, :] = (mine.astype(F32) + wcore[n, rows, :].astype(F32)).astype(BF16)
        return to_cols(4 + n, lambda j: whalf.at[n, at(128 * j, 128, 128), :], lambda d: wcol.at[n, d])

    def w_rows(n, copies):
        wait_all(copies)
        total = whalf[n, at(128 * c, 128, 128), :].astype(F32)
        for d in range(1, 8):
            total = total + wcol[n, d].astype(F32)
        wquarter[n] = total
        return to_rows(1 + n, lambda j: wquarter.at[n, at(8 * j, 8, 8), :], lambda d: wrow.at[n, d])

    def w_rows_back(n, copies):
        wait_all(copies)
        total = wquarter[n, at(8 * k, 8, 8), :]
        for d in range(1, 16):
            total = total + wrow[n, d]
        wfin[n] = total
        wrgat[n, at(8 * k, 8, 8), :] = total
        return to_rows(3 + n, lambda j: wfin.at[n], lambda d: wrgat.at[n, at(8 * k, 8, 8), :])

    def w_cols_back(n, copies):
        wait_all(copies)
        place = at(2048 * n + 1024 * core + 128 * c, 128, 128)
        wgat[place, :] = wrgat[n].astype(BF16)
        return to_cols(7 + n, lambda j: wgat.at[place, :], lambda d: wgat.at[place, :])

    def w_core_back(n, copies):
        wait_all(copies)
        half = wgat.at[at(2048 * n + 1024 * core, 1024, 1024), :]
        cp = remote(half, half, core_s.at[3 + n], core_r.at[3 + n], partner)
        cp.start()
        return cp

    slope_own = sx[1, 0:128, 128:256]
    for a in range(3):
        wsend[768 * a : 768 * a + 768, :] = dot_tn(imc[a + 1, 0:128, :], slope_own).astype(BF16)
    wa = w_core(0)
    for a in range(3):
        wsend[2304 + 384 * a : 2688 + 384 * a, :] = dot_tn(hx[a, 0:128, :], cot[...]).astype(BF16)
    wsend[3456:4096, :] = jnp.zeros((640, 128), BF16)
    wb = w_core(1)
    out_ref[...] = (
        dot(hx[0, 0:128, :], k2[0:384, :])
        + dot(hx[1, 0:128, :], k2[384:768, :])
        + dot(hx[2, 0:128, :], k2[768:1152, :])
    ).astype(BF16)

    wait_all(up_copies)
    scaled = (up_t[...].astype(F32) * inv_ref[0:1, :]).astype(BF16)
    u_ext[0:32, :] = scaled
    inner = jnp.sum(scaled.astype(F32) * att_t[...].astype(F32), axis=0, keepdims=True)
    inner_high = inner.astype(BF16).astype(F32)
    extra = lax.broadcasted_iota(jnp.int32, (16, 1024), 0)
    u_ext[32:48, :] = jnp.where(
        extra == 0, -inner_high, jnp.where(extra == 1, inner_high - inner, 0.0)
    ).astype(BF16)

    def backward(ib):
        lanes = slice(256 * ib, 256 * ib + 256)
        u_block = u_ext[:, lanes]
        for jc in range(8):
            rows = slice(128 * jc, 128 * jc + 128)
            slopes = dot(vext[rows, :], u_block)
            d_ref[rows, lanes] = (e_ref[rows, lanes].astype(F32) * slopes).astype(BF16)
        g_t[0:16, lanes] = (dot(qkv[16:32, :], d_ref[:, lanes]) * 0.25).astype(BF16)

    wa = w_cols(0, wa)
    backward(0)
    wb = w_cols(1, wb)
    backward(1)
    backward(2)
    backward(3)
    g_t[32:64, :] = dot_nt(u_ext[0:32, :], e_ref[...]).astype(BF16)
    g_t[16:32, :] = (dot_nt(qkv[0:16, :], d_ref[...]) * 0.25).astype(BF16)

    wait_all(feat_copies)
    turned = dot(g_t[...], featx[...])
    pblock[0:64, :] = turned[:, 0:128]
    pblock[64:128, :] = turned[:, 128:256]
    p2 = to_rows(0, lambda j: pblock.at[at(8 * j, 8, 8), :], lambda d: prow.at[d])
    g_copies = to_cols(6, lambda j: g_t.at[:, at(128 * j, 128, 128)], lambda d: g_recv.at[at(64 * c, 64, 64), :])
    g_recv[at(64 * c, 64, 64), :] = g_t[:, my_lanes]

    wa = w_rows(0, wa)
    wb = w_rows(1, wb)
    wait_all(p2)
    total = pblock[at(8 * k, 8, 8), :]
    for d in range(1, 16):
        total = total + prow[d]
    pfin[...] = total
    p3 = remote(pfin, pcore, core_s.at[2], core_r.at[2], partner)
    p3.start()
    wa = w_rows_back(0, wa)
    p3.wait()
    pmine[...] = pfin[...] + pcore[...]
    p4 = to_rows(5, lambda j: pmine, lambda d: prgat.at[at(8 * k, 8, 8), :])
    prgat[at(8 * k, 8, 8), :] = pmine[...]
    wb = w_rows_back(1, wb)

    wait_all(g_copies)
    parts = []
    for first, size in ((0, 16), (16, 16), (32, 32)):
        for h in range(8):
            parts.append(g_recv[64 * h + first : 64 * h + first + size, :].astype(F32))
    grads = jnp.transpose(jnp.concatenate(parts)).astype(BF16)
    ig_ref[...] = dot_nt(grads, proj[...]).astype(BF16)

    wa = w_cols_back(0, wa)
    wait_all(p4)
    pgat[at(128 * c, 128, 128), :] = prgat[...].astype(BF16)
    block = pgat.at[at(128 * c, 128, 128), :]
    p5 = to_cols(9, lambda j: block, lambda d: block)
    wb = w_cols_back(1, wb)
    wa = w_core_back(0, wa)
    wait_all(p5)
    for h in range(8):
        for side in range(2):
            base = 128 * h + 64 * side
            lanes = slice(128 * side, 128 * side + 128)
            p_out[16 * h : 16 * h + 16, lanes] = pgat[base : base + 16, :]
            p_out[128 + 16 * h : 144 + 16 * h, lanes] = pgat[base + 16 : base + 32, :]
            p_out[256 + 32 * h : 288 + 32 * h, lanes] = pgat[base + 32 : base + 64, :]
    wb = w_core_back(1, wb)
    wa.wait()
    w_out[0:2048, :] = wgat[0:2048, :]
    wb.wait()
    w_out[2048:4096, :] = wgat[2048:4096, :]


def finish_kernel(out_in, ig_in, w_in, p_in, out_ref, ig_ref, proj_ref, first_ref, second_ref):
    factor = 1.0 / math.sqrt(HEIGHT * WIDTH)
    out_ref[...] = out_in[...]
    ig_ref[...] = ig_in[...]
    proj_ref[...] = jnp.transpose(p_in[...].astype(F32)) * factor
    first_ref[...] = w_in[0:2304, :].astype(F32) * factor
    second_ref[...] = w_in[2304:3456, :].astype(F32) * factor


def body(features, projection, first_kernel, second_kernel, cotangent):
    vm = pltpu.VMEM
    dma = pltpu.SemaphoreType.DMA
    out, grad, weights, proj_grad = pl.pallas_call(
        block_kernel,
        out_shape=(
            jax.ShapeDtypeStruct((128, 128), BF16),
            jax.ShapeDtypeStruct((128, 256), BF16),
            jax.ShapeDtypeStruct((4096, 128), BF16),
            jax.ShapeDtypeStruct((512, 256), BF16),
        ),
        in_specs=[pl.BlockSpec(memory_space=pltpu.HBM)] * 5,
        out_specs=[pl.BlockSpec(memory_space=vm)] * 4,
        scratch_shapes=[
            vm((128, 256), BF16), vm((256, 512), BF16), vm((2304, 128), BF16), vm((1152, 128), BF16), vm((128, 128), BF16),
            vm((512, 128), BF16), vm((64, 1024), BF16), vm((32, 1024), BF16), vm((8, 1024), F32),
            vm((2, 1024, 256), F32), vm((1024, 1024), BF16), vm((1024, 1024), BF16),
            vm((1024, 16), BF16), vm((1024, 48), BF16), vm((48, 1024), BF16),
            vm((8, 32, 256), BF16), vm((256, 256), BF16), vm((5, 144, 256), BF16), vm((5, 144, 768), BF16),
            vm((16, 128), BF16), vm((16, 128), BF16), vm((5, 144, 128), BF16), vm((5, 144, 384), BF16),
            vm((3, 384, 128), BF16), vm((3, 384, 256), BF16), vm((3, 144, 128), F32),
            vm((3, 144, 384), BF16), vm((3, 144, 384), BF16),
            vm((256, 128), BF16), vm((32, 1024), BF16), vm((48, 1024), BF16),
            vm((64, 1024), BF16), vm((512, 128), BF16), vm((1024, 256), BF16),
            vm((4096, 128), BF16), vm((2, 1024, 128), BF16), vm((2, 1024, 128), BF16), vm((2, 8, 128, 128), BF16),
            vm((2, 128, 128), F32), vm((2, 16, 8, 128), F32), vm((2, 8, 128), F32), vm((2, 128, 128), F32), vm((4096, 128), BF16),
            vm((128, 128), F32), vm((16, 8, 128), F32), vm((8, 128), F32), vm((8, 128), F32),
            vm((128, 128), F32), vm((8, 128), F32), vm((1024, 128), BF16),
            dma((5,)), dma((5,)), dma((10, 8)), dma((10, 8)), dma((6, 16)), dma((6, 16)), dma((3, 4)), dma((3, 4)), dma((5,)),
        ],
        compiler_params=pltpu.CompilerParams(
            collective_id=0, has_side_effects=True, vmem_limit_bytes=32 * 1024 * 1024
        ),
    )(
        *(
            pltpu.with_memory_space_constraint(x, pltpu.HBM)
            for x in (
                features.reshape(128, 256),
                projection,
                first_kernel.reshape(2304, 128),
                second_kernel.reshape(1152, 128),
                cotangent.reshape(128, 128),
            )
        )
    )
    out, grad, proj_grad, first, second = pl.pallas_call(
        finish_kernel,
        out_shape=(
            jax.ShapeDtypeStruct((128, 128), BF16),
            jax.ShapeDtypeStruct((128, 256), BF16),
            jax.ShapeDtypeStruct((256, 512), F32),
            jax.ShapeDtypeStruct((2304, 128), F32),
            jax.ShapeDtypeStruct((1152, 128), F32),
        ),
        in_specs=[pl.BlockSpec(memory_space=vm)] * 4,
        out_specs=[pl.BlockSpec(memory_space=vm)] * 5,
        compiler_params=pltpu.CompilerParams(vmem_limit_bytes=16 * 1024 * 1024),
    )(out, grad, weights, proj_grad)
    return (
        out.reshape(1, 128, 128),
        grad.reshape(1, 128, 256),
        proj_grad,
        first.reshape(3, 3, 256, 128),
        second.reshape(3, 3, 128, 128),
    )


def solution(mesh):
    placed = (P("rows", "cols", None), P(), P(), P(), P("rows", "cols", None))
    return jax.shard_map(
        body,
        mesh=mesh,
        in_specs=placed,
        out_specs=(P("rows", "cols", None), P("rows", "cols", None), P(), P(), P()),
        check_vma=False,
    )
```

```python
import math

import jax
import jax.numpy as jnp
from jax import lax
from jax.experimental import pallas as pl
from jax.experimental.pallas import tpu as pltpu
from jax.sharding import PartitionSpec as P

MESH = pl.DeviceIdType.MESH
F32 = jnp.float32
BF16 = jnp.bfloat16
HEIGHT = 32
WIDTH = 1024


def remote(src, dst, send_sem, recv_sem, device):
    return pltpu.make_async_remote_copy(
        src_ref=src, dst_ref=dst, send_sem=send_sem, recv_sem=recv_sem,
        device_id=device, device_id_type=MESH,
    )


def at(start, size, align):
    return pl.ds(pl.multiple_of(start, align), size)


def dot(a, b):
    return jnp.dot(a, b, preferred_element_type=F32)


def dot_nt(a, b):
    return lax.dot_general(a, b, (((1,), (1,)), ((), ())), preferred_element_type=F32)


def dot_tn(a, b):
    return lax.dot_general(a, b, (((0,), (0,)), ((), ())), preferred_element_type=F32)


def shifted(x):
    return pltpu.roll(x, 1, 0), x, pltpu.roll(x, 143, 0)


def wait_all(copies):
    for cp in copies:
        cp.wait()


def block_kernel(
    feat_in, proj_in, k1_in, k2_in, cot_in, out_ref, ig_ref, w_out, p_out,
    feat, proj, k1, k2, cot,
    qkv_send, qkv, att_t, inv_ref, s_ref, e_ref, d_ref, kmat, vext, vext_t,
    att_send, att_recv, attx, imc, cot_l, cot_r, cotx, cim, k2t, k1t, tc,
    hx, sx, up_send, up_t, u_ext, g_t, g_recv, featx,
    att_near, slope_own, slope_row, hid_send, hid_row, cot_row, a9, h9,
    wsend, wcore, whalf, wrow, wfin, wrgat, wgat,
    pblock, prow, pfin, pcore, prgat, pmine, pgat,
    core_s, core_r, col_s, col_r, row_s, row_r, halo_s, halo_r, load_s,
):
    r = lax.axis_index("rows")
    c = lax.axis_index("cols")
    core = r % 2
    k = r // 2
    partner = (r + 1 - 2 * core, c)

    def col_dev(d):
        return (r, (c + d) % 8)

    def row_dev(d):
        return (2 * ((k + d) % 16) + core, c)

    def near(d):
        return ((r + d + 32) % 32, c)

    def to_cols(kind, src_of, dst):
        copies = []
        for d in range(1, 8):
            cp = remote(src_of((c + d) % 8), dst(d), col_s.at[kind, d], col_r.at[kind, d], col_dev(d))
            cp.start()
            copies.append(cp)
        return copies

    def to_rows(kind, src_of, dst):
        copies = []
        for d in range(1, 16):
            cp = remote(src_of((k + d) % 16), dst(d), row_s.at[kind, d], row_r.at[kind, d], row_dev(d))
            cp.start()
            copies.append(cp)
        return copies

    def to_near(kind, src, slots):
        copies = []
        for n, d in enumerate((-2, -1, 1, 2)):
            cp = remote(src, slots.at[2 - d], halo_s.at[kind, n], halo_r.at[kind, n], near(d))
            cp.start()
            copies.append(cp)
        return copies

    barrier = pltpu.get_barrier_semaphore()
    pl.semaphore_signal(barrier, inc=1, device_id=partner, device_id_type=MESH)
    pl.semaphore_signal(barrier, inc=1, device_id=near(2 * core - 1), device_id_type=MESH)
    for d in range(1, 8):
        pl.semaphore_signal(barrier, inc=1, device_id=col_dev(d), device_id_type=MESH)
    for d in range(1, 16):
        pl.semaphore_signal(barrier, inc=1, device_id=row_dev(d), device_id_type=MESH)

    loads = []
    for n, (src, dst) in enumerate(
        ((feat_in, feat), (proj_in, proj), (cot_in, cot), (k2_in, k2), (k1_in, k1))
    ):
        cp = pltpu.make_async_copy(src, dst, load_s.at[n])
        cp.start()
        loads.append(cp)

    wait_all(loads[0:2])
    packed = jnp.transpose(dot(feat[...], proj[...])).astype(BF16)
    for h in range(8):
        qkv_send[64 * h : 64 * h + 16, :] = packed[16 * h : 16 * h + 16]
        qkv_send[64 * h + 16 : 64 * h + 32, :] = packed[128 + 16 * h : 144 + 16 * h]
        qkv_send[64 * h + 32 : 64 * h + 64, :] = packed[256 + 32 * h : 288 + 32 * h]
    wait_all(loads[2:5])
    pl.semaphore_wait(barrier, 24)
    my_lanes = at(128 * c, 128, 128)
    qkv_copies = to_cols(
        0, lambda j: qkv_send.at[at(64 * j, 64, 64), :], lambda d: qkv.at[:, my_lanes]
    )
    left = remote(cot.at[112:128], cot_l, halo_s.at[2, 0], halo_r.at[2, 0], col_dev(1))
    left.start()
    right = remote(cot.at[0:16], cot_r, halo_s.at[2, 1], halo_r.at[2, 1], col_dev(7))
    right.start()
    qkv[:, my_lanes] = qkv_send[at(64 * c, 64, 64), :]
    for a in range(3):
        for b in range(3):
            n = 3 * a + b
            k2t[a, 128 * b : 128 * b + 128, :] = jnp.transpose(
                k2[128 * n : 128 * n + 128, :].astype(F32)
            ).astype(BF16)
            k1t[a, 128 * b : 128 * b + 128, :] = jnp.transpose(
                k1[256 * n : 256 * n + 256, :].astype(F32)
            ).astype(BF16)
    index = lax.broadcasted_iota(jnp.int32, (144, 128), 0)
    low_end = 136 - 8 * (c // 7)
    high_start = 136 + 8 * ((7 - c) // 7)

    def in_image(row):
        return jnp.where((row >= 0) & (row < HEIGHT), 1, 0)

    left.wait()
    right.wait()
    cotx[2] = jnp.where(
        (index < low_end) | (index >= high_start),
        jnp.concatenate([cot[...].astype(F32), cot_r[0:8, :].astype(F32), cot_l[8:16, :].astype(F32)]),
        0.0,
    ).astype(BF16)
    cot_copies = to_near(0, cotx.at[2], cotx)
    wait_all(qkv_copies)

    kmat[...] = (jnp.transpose(qkv[16:32, :].astype(F32)) * 0.25).astype(BF16)
    vext_t[0:32, :] = qkv[32:64, :]
    extra = lax.broadcasted_iota(jnp.int32, (16, 1024), 0)
    vext_t[32:48, :] = jnp.where(extra < 2, 1.0, 0.0).astype(BF16)
    vext[...] = jnp.transpose(vext_t[...].astype(F32)).astype(BF16)
    lane = lax.broadcasted_iota(jnp.int32, (32, 128), 1)
    zero = jnp.zeros((32, 128), F32)

    def send_attended(j):
        after = att_t[:, 128 * j + 128 : 128 * j + 256].astype(F32) if j < 7 else zero
        before = att_t[:, 128 * j - 128 : 128 * j].astype(F32) if j > 0 else zero
        att_send[j, :, 0:128] = att_t[:, 128 * j : 128 * j + 128]
        att_send[j, :, 128:256] = jnp.where(lane < 64, after, before).astype(BF16)

        @pl.when(c != j)
        def _():
            d = (j - c + 8) % 8
            remote(
                att_send.at[j], att_recv.at[at(32 * c, 32, 32), :], col_s.at[2, d], col_r.at[2, d], (r, j)
            ).start()

    for ib in range(4):
        lanes = slice(256 * ib, 256 * ib + 256)
        q_block = qkv[0:16, lanes]
        top = None
        for jc in range(8):
            s = dot(kmat[128 * jc : 128 * jc + 128, :], q_block)
            s_ref[ib % 2, 128 * jc : 128 * jc + 128, :] = s
            part = jnp.max(s.reshape(16, 8, 256), axis=0)
            top = part if top is None else jnp.maximum(top, part)
        top = jnp.max(top, axis=0, keepdims=True)
        for jc in range(8):
            rows = slice(128 * jc, 128 * jc + 128)
            e_ref[rows, lanes] = jnp.exp(s_ref[ib % 2, rows, :] - top).astype(BF16)
        weighted = dot(vext_t[...], e_ref[:, lanes])
        inverse = 1.0 / weighted[32:33, :]
        inv_ref[0:1, lanes] = inverse
        att_t[:, lanes] = (weighted[0:32, :] * inverse).astype(BF16)
        for j in ((0,), (1, 2), (3, 4), (5, 6, 7))[ib]:
            send_attended(j)

    row_copies = []
    for n, d in enumerate((-1, 1)):
        cp = remote(att_t, att_near.at[n], halo_s.at[2, 2 + n], halo_r.at[2, 2 + n], near(d))
        cp.start()
        row_copies.append(cp)
    feat_copies = to_cols(1, lambda j: feat, lambda d: featx.at[at(128 * c, 128, 128), :])
    featx[at(128 * c, 128, 128), :] = feat[...]
    cot_row_copies = to_cols(8, lambda j: cot, lambda d: cot_row.at[at(128 * c, 128, 128), :])
    cot_row[at(128 * c, 128, 128), :] = cot[...]
    att_recv[at(32 * c, 32, 32), :] = att_send[c]

    wait_all(cot_copies)
    for slot in range(5):
        x = cotx[slot].astype(F32) * in_image(r - 2 + slot).astype(F32)
        low, mid, high = shifted(x)
        cim[slot, :, 0:128] = high.astype(BF16)
        cim[slot, :, 128:256] = mid.astype(BF16)
        cim[slot, :, 256:384] = low.astype(BF16)
    for t in range(3):
        tc[t] = (
            dot(cim[t + 2], k2t[0]) + dot(cim[t + 1], k2t[1]) + dot(cim[t], k2t[2])
        )

    for d in range(1, 8):
        remote(
            att_send.at[(c + d) % 8], att_recv.at[at(32 * c, 32, 32), :],
            col_s.at[2, d], col_r.at[2, d], col_dev(d),
        ).wait()
    turned = jnp.transpose(att_recv[...].astype(F32))
    attx[2] = jnp.concatenate([turned[0:136], turned[248:256]]).astype(BF16)
    near_copies = to_near(1, attx.at[2], attx)

    def columns(slot):
        x = attx[slot].astype(F32) * in_image(r - 2 + slot).astype(F32)
        low, mid, high = shifted(x)
        imc[slot, :, 0:256] = low.astype(BF16)
        imc[slot, :, 256:512] = mid.astype(BF16)
        imc[slot, :, 512:768] = high.astype(BF16)

    columns(2)
    column = lax.broadcasted_iota(jnp.int32, (48, 1024), 1)

    def lane_shifted(x):
        n = x.shape[0]
        low = jnp.where(column[0:n] == 0, 0.0, pltpu.roll(x, 1, 1))
        high = jnp.where(column[0:n] == 1023, 0.0, pltpu.roll(x, 1023, 1))
        return low.astype(BF16), x.astype(BF16), high.astype(BF16)

    wait_all(row_copies)
    for a in range(3):
        x = (att_near[1], att_t[...], att_near[0])[a].astype(F32) * in_image(r - 1 + a).astype(F32)
        for b, y in enumerate(lane_shifted(x)):
            a9[96 * a + 32 * b : 96 * a + 32 * b + 32, :] = y
    wait_all(near_copies)
    for slot in (0, 1, 3, 4):
        columns(slot)

    for t in range(3):
        pre = (
            dot(imc[t], k1[0:768, :])
            + dot(imc[t + 1], k1[768:1536, :])
            + dot(imc[t + 2], k1[1536:2304, :])
        )
        valid = in_image(r - 1 + t)
        keep = (index < low_end * valid) | (index >= 144 - (144 - high_start) * valid)
        sigma = 1.0 / (1.0 + jnp.exp(-pre))
        slope = jnp.where(keep, tc[t] * (sigma * (1.0 + pre * (1.0 - sigma))), 0.0)
        low, mid, high = shifted(slope)
        sx[t, :, 0:128] = high.astype(BF16)
        sx[t, :, 128:256] = mid.astype(BF16)
        sx[t, :, 256:384] = low.astype(BF16)
        if t == 1:
            slope_own[...] = slope[0:128].astype(BF16)
            slope_copies = to_cols(4, lambda j: slope_own, lambda d: slope_row.at[at(128 * c, 128, 128), :])
        hidden = jnp.where(keep, pre * sigma, 0.0)
        turned = jnp.transpose(hidden[0:128]).astype(BF16)
        for j in range(8):
            hid_send[j, 16 * t : 16 * t + 16, :] = turned[16 * j : 16 * j + 16]
        low, mid, high = shifted(hidden)
        hx[t, :, 0:128] = low.astype(BF16)
        hx[t, :, 128:256] = mid.astype(BF16)
        hx[t, :, 256:384] = high.astype(BF16)

    hid_copies = to_cols(5, lambda j: hid_send.at[j], lambda d: hid_row.at[:, my_lanes])

    upstream = (
        dot(sx[2, 0:128, :], k1t[0]) + dot(sx[1, 0:128, :], k1t[1]) + dot(sx[0, 0:128, :], k1t[2])
    )
    up_send[...] = jnp.transpose(upstream).astype(BF16)
    up_copies = to_cols(3, lambda j: up_send.at[at(32 * j, 32, 32), :], lambda d: up_t.at[:, my_lanes])
    up_t[:, my_lanes] = up_send[at(32 * c, 32, 32), :]

    out_ref[...] = (
        dot(hx[0, 0:128, :], k2[0:384, :])
        + dot(hx[1, 0:128, :], k2[384:768, :])
        + dot(hx[2, 0:128, :], k2[768:1152, :])
    ).astype(BF16)

    slope_row[at(128 * c, 128, 128), :] = slope_own[...]
    hid_row[:, my_lanes] = hid_send[c]
    wait_all(slope_copies)
    wait_all(cot_row_copies)
    wait_all(hid_copies)
    wsend[0:288, :] = dot(a9[...], slope_row[...]).astype(BF16)
    for b, y in enumerate(lane_shifted(hid_row[...].astype(F32))):
        for a in range(3):
            h9[48 * a + 16 * b : 48 * a + 16 * b + 16, :] = y[16 * a : 16 * a + 16]
    wsend[288:432, :] = dot(h9[...], cot_row[...]).astype(BF16)
    wsend[432:480, :] = jnp.zeros((48, 128), BF16)
    w_copy = remote(wsend.at[at(224 * (1 - core), 256, 32)], wcore, core_s.at[0], core_r.at[0], partner)
    w_copy.start()

    wait_all(up_copies)
    scaled = (up_t[...].astype(F32) * inv_ref[0:1, :]).astype(BF16)
    u_ext[0:32, :] = scaled
    inner = jnp.sum(scaled.astype(F32) * att_t[...].astype(F32), axis=0, keepdims=True)
    inner_high = inner.astype(BF16).astype(F32)
    extra = lax.broadcasted_iota(jnp.int32, (16, 1024), 0)
    u_ext[32:48, :] = jnp.where(
        extra == 0, -inner_high, jnp.where(extra == 1, inner_high - inner, 0.0)
    ).astype(BF16)

    def backward(ib):
        lanes = slice(256 * ib, 256 * ib + 256)
        u_block = u_ext[:, lanes]
        for jc in range(8):
            rows = slice(128 * jc, 128 * jc + 128)
            slopes = dot(vext[rows, :], u_block)
            d_ref[rows, lanes] = (e_ref[rows, lanes].astype(F32) * slopes).astype(BF16)
        g_t[0:16, lanes] = (dot(qkv[16:32, :], d_ref[:, lanes]) * 0.25).astype(BF16)

    w_copy.wait()
    whalf[...] = (wsend[at(224 * core, 256, 32), :].astype(F32) + wcore[...].astype(F32)).astype(BF16)
    w_copies = to_rows(1, lambda j: whalf.at[at(16 * j, 16, 16), :], lambda d: wrow.at[d])
    backward(0)
    backward(1)
    backward(2)
    backward(3)
    g_t[32:64, :] = dot_nt(u_ext[0:32, :], e_ref[...]).astype(BF16)
    g_t[16:32, :] = (dot_nt(qkv[0:16, :], d_ref[...]) * 0.25).astype(BF16)

    wait_all(feat_copies)
    turned = dot(g_t[...], featx[...])
    pblock[0:64, :] = turned[:, 0:128]
    pblock[64:128, :] = turned[:, 128:256]
    p2 = to_rows(0, lambda j: pblock.at[at(8 * j, 8, 8), :], lambda d: prow.at[d])
    g_copies = to_cols(6, lambda j: g_t.at[:, at(128 * j, 128, 128)], lambda d: g_recv.at[at(64 * c, 64, 64), :])
    g_recv[at(64 * c, 64, 64), :] = g_t[:, my_lanes]

    wait_all(w_copies)
    total = whalf[at(16 * k, 16, 16), :].astype(F32)
    for d in range(1, 16):
        total = total + wrow[d].astype(F32)
    wfin[...] = total.astype(BF16)
    wrgat[at(16 * k, 16, 16), :] = wfin[...]
    w_copies = to_rows(2, lambda j: wfin, lambda d: wrgat.at[at(16 * k, 16, 16), :])
    wait_all(p2)
    total = pblock[at(8 * k, 8, 8), :]
    for d in range(1, 16):
        total = total + prow[d]
    pfin[...] = total
    p3 = remote(pfin, pcore, core_s.at[2], core_r.at[2], partner)
    p3.start()
    p3.wait()
    pmine[...] = pfin[...] + pcore[...]
    p4 = to_rows(3, lambda j: pmine, lambda d: prgat.at[at(8 * k, 8, 8), :])
    prgat[at(8 * k, 8, 8), :] = pmine[...]
    wait_all(w_copies)
    back = []
    for m in range(2):
        place = at(112 * c, 112, 16)
        wgat[core, m, place, :] = wrgat[112 * m : 112 * m + 112, :]
        back.append(to_cols(7 if m == 0 else 10, lambda j: wgat.at[core, m, place, :], lambda d: wgat.at[core, m, place, :]))
    wait_all(g_copies)
    parts = []
    for first, size in ((0, 16), (16, 16), (32, 32)):
        for h in range(8):
            parts.append(g_recv[64 * h + first : 64 * h + first + size, :].astype(F32))
    grads = jnp.transpose(jnp.concatenate(parts)).astype(BF16)
    ig_ref[...] = dot_nt(grads, proj[...]).astype(BF16)

    wait_all(p4)
    pgat[at(128 * c, 128, 128), :] = prgat[...].astype(BF16)
    block = pgat.at[at(128 * c, 128, 128), :]
    p5 = to_cols(9, lambda j: block, lambda d: block)
    swap = []
    for m in range(2):
        wait_all(back[m])
        cp = remote(wgat.at[core, m], wgat.at[core, m], core_s.at[3 + m], core_r.at[3 + m], partner)
        cp.start()
        swap.append(cp)
    wait_all(p5)
    for h in range(8):
        for side in range(2):
            base = 128 * h + 64 * side
            lanes = slice(128 * side, 128 * side + 128)
            p_out[16 * h : 16 * h + 16, lanes] = pgat[base : base + 16, :]
            p_out[128 + 16 * h : 144 + 16 * h, lanes] = pgat[base + 16 : base + 32, :]
            p_out[256 + 32 * h : 288 + 32 * h, lanes] = pgat[base + 32 : base + 64, :]
    for cp in swap:
        cp.wait()
    w_out[...] = wgat[...]


def finish_kernel(out_in, ig_in, w_in, p_in, out_ref, ig_ref, proj_ref, first_ref, second_ref):
    factor = 1.0 / math.sqrt(HEIGHT * WIDTH)
    out_ref[...] = out_in[...]
    ig_ref[...] = ig_in[...]
    proj_ref[...] = jnp.transpose(p_in[...].astype(F32)) * factor
    for h in range(8):
        for n in range(27):
            q, row = n // 7, 112 * h + 16 * (n % 7)
            values = w_in[q // 2, q % 2, row : row + 16, :].astype(F32) * factor
            if n < 18:
                start = 256 * (n // 2) + 32 * h + 16 * (n % 2)
                first_ref[start : start + 16, :] = values
            else:
                start = 128 * (n - 18) + 16 * h
                second_ref[start : start + 16, :] = values


def body(features, projection, first_kernel, second_kernel, cotangent):
    vm = pltpu.VMEM
    dma = pltpu.SemaphoreType.DMA
    out, grad, weights, proj_grad = pl.pallas_call(
        block_kernel,
        out_shape=(
            jax.ShapeDtypeStruct((128, 128), BF16),
            jax.ShapeDtypeStruct((128, 256), BF16),
            jax.ShapeDtypeStruct((2, 2, 896, 128), BF16),
            jax.ShapeDtypeStruct((512, 256), BF16),
        ),
        in_specs=[pl.BlockSpec(memory_space=pltpu.HBM)] * 5,
        out_specs=[pl.BlockSpec(memory_space=vm)] * 4,
        scratch_shapes=[
            vm((128, 256), BF16), vm((256, 512), BF16), vm((2304, 128), BF16), vm((1152, 128), BF16), vm((128, 128), BF16),
            vm((512, 128), BF16), vm((64, 1024), BF16), vm((32, 1024), BF16), vm((8, 1024), F32),
            vm((2, 1024, 256), F32), vm((1024, 1024), BF16), vm((1024, 1024), BF16),
            vm((1024, 16), BF16), vm((1024, 48), BF16), vm((48, 1024), BF16),
            vm((8, 32, 256), BF16), vm((256, 256), BF16), vm((5, 144, 256), BF16), vm((5, 144, 768), BF16),
            vm((16, 128), BF16), vm((16, 128), BF16), vm((5, 144, 128), BF16), vm((5, 144, 384), BF16),
            vm((3, 384, 128), BF16), vm((3, 384, 256), BF16), vm((3, 144, 128), F32),
            vm((3, 144, 384), BF16), vm((3, 144, 384), BF16),
            vm((256, 128), BF16), vm((32, 1024), BF16), vm((48, 1024), BF16),
            vm((64, 1024), BF16), vm((512, 128), BF16), vm((1024, 256), BF16),
            vm((2, 32, 1024), BF16), vm((128, 128), BF16), vm((1024, 128), BF16), vm((8, 48, 128), BF16),
            vm((48, 1024), BF16), vm((1024, 128), BF16), vm((288, 1024), BF16), vm((144, 1024), BF16),
            vm((480, 128), BF16), vm((256, 128), BF16), vm((256, 128), BF16), vm((16, 16, 128), BF16),
            vm((16, 128), BF16), vm((256, 128), BF16), vm((2, 2, 896, 128), BF16),
            vm((128, 128), F32), vm((16, 8, 128), F32), vm((8, 128), F32), vm((8, 128), F32),
            vm((128, 128), F32), vm((8, 128), F32), vm((1024, 128), BF16),
            dma((5,)), dma((5,)), dma((11, 8)), dma((11, 8)), dma((4, 16)), dma((4, 16)), dma((3, 4)), dma((3, 4)), dma((5,)),
        ],
        compiler_params=pltpu.CompilerParams(
            collective_id=0, has_side_effects=True, vmem_limit_bytes=32 * 1024 * 1024
        ),
    )(
        *(
            pltpu.with_memory_space_constraint(x, pltpu.HBM)
            for x in (
                features.reshape(128, 256),
                projection,
                first_kernel.reshape(2304, 128),
                second_kernel.reshape(1152, 128),
                cotangent.reshape(128, 128),
            )
        )
    )
    out, grad, proj_grad, first, second = pl.pallas_call(
        finish_kernel,
        out_shape=(
            jax.ShapeDtypeStruct((128, 128), BF16),
            jax.ShapeDtypeStruct((128, 256), BF16),
            jax.ShapeDtypeStruct((256, 512), F32),
            jax.ShapeDtypeStruct((2304, 128), F32),
            jax.ShapeDtypeStruct((1152, 128), F32),
        ),
        in_specs=[pl.BlockSpec(memory_space=vm)] * 4,
        out_specs=[pl.BlockSpec(memory_space=vm)] * 5,
        compiler_params=pltpu.CompilerParams(vmem_limit_bytes=16 * 1024 * 1024),
    )(out, grad, weights, proj_grad)
    return (
        out.reshape(1, 128, 128),
        grad.reshape(1, 128, 256),
        proj_grad,
        first.reshape(3, 3, 256, 128),
        second.reshape(3, 3, 128, 128),
    )


def solution(mesh):
    placed = (P("rows", "cols", None), P(), P(), P(), P("rows", "cols", None))
    return jax.shard_map(
        body,
        mesh=mesh,
        in_specs=placed,
        out_specs=(P("rows", "cols", None), P("rows", "cols", None), P(), P(), P()),
        check_vma=False,
    )
```

```python
import math

import jax
import jax.numpy as jnp
from jax import lax
from jax.experimental import pallas as pl
from jax.experimental.pallas import tpu as pltpu
from jax.sharding import PartitionSpec as P

MESH = pl.DeviceIdType.MESH
F32 = jnp.float32
BF16 = jnp.bfloat16
HEIGHT = 32
WIDTH = 1024


def remote(src, dst, send_sem, recv_sem, device):
    return pltpu.make_async_remote_copy(
        src_ref=src, dst_ref=dst, send_sem=send_sem, recv_sem=recv_sem,
        device_id=device, device_id_type=MESH,
    )


def at(start, size, align):
    return pl.ds(pl.multiple_of(start, align), size)


def dot(a, b):
    return jnp.dot(a, b, preferred_element_type=F32)


def dot_nt(a, b):
    return lax.dot_general(a, b, (((1,), (1,)), ((), ())), preferred_element_type=F32)


def dot_tn(a, b):
    return lax.dot_general(a, b, (((0,), (0,)), ((), ())), preferred_element_type=F32)


def shifted(x):
    return pltpu.roll(x, 1, 0), x, pltpu.roll(x, 143, 0)


def wait_all(copies):
    for cp in copies:
        cp.wait()


def block_kernel(
    feat_in, proj_in, k1_in, k2_in, cot_in, out_ref, ig_ref, w_out, p_out,
    feat, proj, k1, k2, cot,
    qkv_send, qkv, att_t, inv_ref, s_ref, e_ref, d_ref, kmat, vext, vext_t,
    att_send, att_recv, attx, imc, cot_l, cot_r, cotx, cim, k2t, k1t, tc,
    hx, sx, up_send, up_t, u_ext, g_t, g_recv, featx,
    att_near, slope_own, slope_row, hid_send, hid_row, cot_row, a9, h9,
    wsend, wcore, whalf, wrow, wfin, wrgat, wgat,
    pblock, prow, pfin, pcore, prgat, pmine, pgat,
    core_s, core_r, col_s, col_r, row_s, row_r, halo_s, halo_r, load_s,
):
    r = lax.axis_index("rows")
    c = lax.axis_index("cols")
    core = r % 2
    k = r // 2
    partner = (r + 1 - 2 * core, c)

    def col_dev(d):
        return (r, (c + d) % 8)

    def row_dev(d):
        return (2 * ((k + d) % 16) + core, c)

    def near(d):
        return ((r + d + 32) % 32, c)

    def to_cols(kind, src_of, dst):
        copies = []
        for d in range(1, 8):
            cp = remote(src_of((c + d) % 8), dst(d), col_s.at[kind, d], col_r.at[kind, d], col_dev(d))
            cp.start()
            copies.append(cp)
        return copies

    def to_rows(kind, src_of, dst):
        copies = []
        for d in range(1, 16):
            cp = remote(src_of((k + d) % 16), dst(d), row_s.at[kind, d], row_r.at[kind, d], row_dev(d))
            cp.start()
            copies.append(cp)
        return copies

    def to_near(kind, src, slots):
        copies = []
        for n, d in enumerate((-2, -1, 1, 2)):
            cp = remote(src, slots.at[2 - d], halo_s.at[kind, n], halo_r.at[kind, n], near(d))
            cp.start()
            copies.append(cp)
        return copies

    barrier = pltpu.get_barrier_semaphore()
    pl.semaphore_signal(barrier, inc=1, device_id=partner, device_id_type=MESH)
    pl.semaphore_signal(barrier, inc=1, device_id=near(2 * core - 1), device_id_type=MESH)
    for d in range(1, 8):
        pl.semaphore_signal(barrier, inc=1, device_id=col_dev(d), device_id_type=MESH)
    for d in range(1, 16):
        pl.semaphore_signal(barrier, inc=1, device_id=row_dev(d), device_id_type=MESH)

    loads = []
    for n, (src, dst) in enumerate(
        ((feat_in, feat), (proj_in, proj), (cot_in, cot), (k2_in, k2), (k1_in, k1))
    ):
        cp = pltpu.make_async_copy(src, dst, load_s.at[n])
        cp.start()
        loads.append(cp)

    wait_all(loads[0:2])
    packed = jnp.transpose(dot(feat[...], proj[...])).astype(BF16)
    for h in range(8):
        qkv_send[64 * h : 64 * h + 16, :] = packed[16 * h : 16 * h + 16]
        qkv_send[64 * h + 16 : 64 * h + 32, :] = packed[128 + 16 * h : 144 + 16 * h]
        qkv_send[64 * h + 32 : 64 * h + 64, :] = packed[256 + 32 * h : 288 + 32 * h]
    wait_all(loads[2:5])
    pl.semaphore_wait(barrier, 24)
    my_lanes = at(128 * c, 128, 128)
    qkv_copies = to_cols(
        0, lambda j: qkv_send.at[at(64 * j, 64, 64), :], lambda d: qkv.at[:, my_lanes]
    )
    left = remote(cot.at[112:128], cot_l, halo_s.at[2, 0], halo_r.at[2, 0], col_dev(1))
    left.start()
    right = remote(cot.at[0:16], cot_r, halo_s.at[2, 1], halo_r.at[2, 1], col_dev(7))
    right.start()
    qkv[:, my_lanes] = qkv_send[at(64 * c, 64, 64), :]
    for a in range(3):
        for b in range(3):
            n = 3 * a + b
            k2t[a, 128 * b : 128 * b + 128, :] = jnp.transpose(
                k2[128 * n : 128 * n + 128, :].astype(F32)
            ).astype(BF16)
            k1t[a, 128 * b : 128 * b + 128, :] = jnp.transpose(
                k1[256 * n : 256 * n + 256, :].astype(F32)
            ).astype(BF16)
    index = lax.broadcasted_iota(jnp.int32, (144, 128), 0)
    low_end = 136 - 8 * (c // 7)
    high_start = 136 + 8 * ((7 - c) // 7)

    def in_image(row):
        return jnp.where((row >= 0) & (row < HEIGHT), 1, 0)

    left.wait()
    right.wait()
    cotx[2] = jnp.where(
        (index < low_end) | (index >= high_start),
        jnp.concatenate([cot[...].astype(F32), cot_r[0:8, :].astype(F32), cot_l[8:16, :].astype(F32)]),
        0.0,
    ).astype(BF16)
    cot_copies = to_near(0, cotx.at[2], cotx)
    wait_all(qkv_copies)
    cot_row_copies = to_cols(8, lambda j: cot, lambda d: cot_row.at[at(128 * c, 128, 128), :])
    cot_row[at(128 * c, 128, 128), :] = cot[...]

    kmat[...] = (jnp.transpose(qkv[16:32, :].astype(F32)) * 0.25).astype(BF16)
    vext_t[0:32, :] = qkv[32:64, :]
    extra = lax.broadcasted_iota(jnp.int32, (16, 1024), 0)
    vext_t[32:48, :] = jnp.where(extra < 2, 1.0, 0.0).astype(BF16)
    vext[...] = jnp.transpose(vext_t[...].astype(F32)).astype(BF16)
    lane = lax.broadcasted_iota(jnp.int32, (32, 128), 1)
    zero = jnp.zeros((32, 128), F32)

    def send_attended(j):
        after = att_t[:, 128 * j + 128 : 128 * j + 256].astype(F32) if j < 7 else zero
        before = att_t[:, 128 * j - 128 : 128 * j].astype(F32) if j > 0 else zero
        att_send[j, :, 0:128] = att_t[:, 128 * j : 128 * j + 128]
        att_send[j, :, 128:256] = jnp.where(lane < 64, after, before).astype(BF16)

        @pl.when(c != j)
        def _():
            d = (j - c + 8) % 8
            remote(
                att_send.at[j], att_recv.at[at(32 * c, 32, 32), :], col_s.at[2, d], col_r.at[2, d], (r, j)
            ).start()

    for ib in range(4):
        lanes = slice(256 * ib, 256 * ib + 256)
        q_block = qkv[0:16, lanes]
        top = None
        for jc in range(8):
            s = dot(kmat[128 * jc : 128 * jc + 128, :], q_block)
            s_ref[ib % 2, 128 * jc : 128 * jc + 128, :] = s
            part = jnp.max(s.reshape(16, 8, 256), axis=0)
            top = part if top is None else jnp.maximum(top, part)
        top = jnp.max(top, axis=0, keepdims=True)
        for jc in range(8):
            rows = slice(128 * jc, 128 * jc + 128)
            e_ref[rows, lanes] = jnp.exp(s_ref[ib % 2, rows, :] - top).astype(BF16)
        weighted = dot(vext_t[...], e_ref[:, lanes])
        inverse = 1.0 / weighted[32:33, :]
        inv_ref[0:1, lanes] = inverse
        att_t[:, lanes] = (weighted[0:32, :] * inverse).astype(BF16)
        for j in ((0,), (1, 2), (3, 4), (5, 6, 7))[ib]:
            send_attended(j)

    row_copies = []
    for n, d in enumerate((-1, 1)):
        cp = remote(att_t, att_near.at[n], halo_s.at[2, 2 + n], halo_r.at[2, 2 + n], near(d))
        cp.start()
        row_copies.append(cp)
    att_recv[at(32 * c, 32, 32), :] = att_send[c]

    wait_all(cot_copies)
    for slot in range(5):
        x = cotx[slot].astype(F32) * in_image(r - 2 + slot).astype(F32)
        low, mid, high = shifted(x)
        cim[slot, :, 0:128] = high.astype(BF16)
        cim[slot, :, 128:256] = mid.astype(BF16)
        cim[slot, :, 256:384] = low.astype(BF16)
    for t in range(3):
        tc[t] = (
            dot(cim[t + 2], k2t[0]) + dot(cim[t + 1], k2t[1]) + dot(cim[t], k2t[2])
        )

    for d in range(1, 8):
        remote(
            att_send.at[(c + d) % 8], att_recv.at[at(32 * c, 32, 32), :],
            col_s.at[2, d], col_r.at[2, d], col_dev(d),
        ).wait()
    turned = jnp.transpose(att_recv[...].astype(F32))
    attx[2] = jnp.concatenate([turned[0:136], turned[248:256]]).astype(BF16)
    near_copies = to_near(1, attx.at[2], attx)
    feat_copies = to_cols(1, lambda j: feat, lambda d: featx.at[at(128 * c, 128, 128), :])
    featx[at(128 * c, 128, 128), :] = feat[...]

    def columns(slot):
        x = attx[slot].astype(F32) * in_image(r - 2 + slot).astype(F32)
        low, mid, high = shifted(x)
        imc[slot, :, 0:256] = low.astype(BF16)
        imc[slot, :, 256:512] = mid.astype(BF16)
        imc[slot, :, 512:768] = high.astype(BF16)

    columns(2)
    column = lax.broadcasted_iota(jnp.int32, (48, 1024), 1)

    def lane_shifted(x):
        n = x.shape[0]
        low = jnp.where(column[0:n] == 0, 0.0, pltpu.roll(x, 1, 1))
        high = jnp.where(column[0:n] == 1023, 0.0, pltpu.roll(x, 1023, 1))
        return low.astype(BF16), x.astype(BF16), high.astype(BF16)

    wait_all(row_copies)
    for a in range(3):
        x = (att_near[1], att_t[...], att_near[0])[a].astype(F32) * in_image(r - 1 + a).astype(F32)
        for b, y in enumerate(lane_shifted(x)):
            a9[96 * a + 32 * b : 96 * a + 32 * b + 32, :] = y
    wait_all(near_copies)
    for slot in (0, 1, 3, 4):
        columns(slot)

    for t in range(3):
        pre = (
            dot(imc[t], k1[0:768, :])
            + dot(imc[t + 1], k1[768:1536, :])
            + dot(imc[t + 2], k1[1536:2304, :])
        )
        valid = in_image(r - 1 + t)
        keep = (index < low_end * valid) | (index >= 144 - (144 - high_start) * valid)
        sigma = 1.0 / (1.0 + jnp.exp(-pre))
        slope = jnp.where(keep, tc[t] * (sigma * (1.0 + pre * (1.0 - sigma))), 0.0)
        low, mid, high = shifted(slope)
        sx[t, :, 0:128] = high.astype(BF16)
        sx[t, :, 128:256] = mid.astype(BF16)
        sx[t, :, 256:384] = low.astype(BF16)
        if t == 1:
            slope_own[...] = slope[0:128].astype(BF16)
        hidden = jnp.where(keep, pre * sigma, 0.0)
        low, mid, high = shifted(hidden)
        hx[t, :, 0:128] = low.astype(BF16)
        hx[t, :, 128:256] = mid.astype(BF16)
        hx[t, :, 256:384] = high.astype(BF16)

    upstream = (
        dot(sx[2, 0:128, :], k1t[0]) + dot(sx[1, 0:128, :], k1t[1]) + dot(sx[0, 0:128, :], k1t[2])
    )
    up_send[...] = jnp.transpose(upstream).astype(BF16)
    up_copies = to_cols(3, lambda j: up_send.at[at(32 * j, 32, 32), :], lambda d: up_t.at[:, my_lanes])
    up_t[:, my_lanes] = up_send[at(32 * c, 32, 32), :]

    slope_copies = to_cols(4, lambda j: slope_own, lambda d: slope_row.at[at(128 * c, 128, 128), :])
    for t in range(3):
        turned = jnp.transpose(hx[t, 0:128, 128:256].astype(F32)).astype(BF16)
        for j in range(8):
            hid_send[j, 16 * t : 16 * t + 16, :] = turned[16 * j : 16 * j + 16]
    hid_copies = to_cols(5, lambda j: hid_send.at[j], lambda d: hid_row.at[:, my_lanes])
    slope_row[at(128 * c, 128, 128), :] = slope_own[...]
    hid_row[:, my_lanes] = hid_send[c]
    out_ref[...] = (
        dot(hx[0, 0:128, :], k2[0:384, :])
        + dot(hx[1, 0:128, :], k2[384:768, :])
        + dot(hx[2, 0:128, :], k2[768:1152, :])
    ).astype(BF16)

    wait_all(up_copies)
    scaled = (up_t[...].astype(F32) * inv_ref[0:1, :]).astype(BF16)
    u_ext[0:32, :] = scaled
    inner = jnp.sum(scaled.astype(F32) * att_t[...].astype(F32), axis=0, keepdims=True)
    inner_high = inner.astype(BF16).astype(F32)
    extra = lax.broadcasted_iota(jnp.int32, (16, 1024), 0)
    u_ext[32:48, :] = jnp.where(
        extra == 0, -inner_high, jnp.where(extra == 1, inner_high - inner, 0.0)
    ).astype(BF16)

    def backward(ib):
        lanes = slice(256 * ib, 256 * ib + 256)
        u_block = u_ext[:, lanes]
        for jc in range(8):
            rows = slice(128 * jc, 128 * jc + 128)
            slopes = dot(vext[rows, :], u_block)
            d_ref[rows, lanes] = (e_ref[rows, lanes].astype(F32) * slopes).astype(BF16)
        g_t[0:16, lanes] = (dot(qkv[16:32, :], d_ref[:, lanes]) * 0.25).astype(BF16)

    backward(0)
    backward(1)
    backward(2)
    backward(3)

    wait_all(slope_copies)
    wait_all(cot_row_copies)
    wait_all(hid_copies)
    wsend[0:288, :] = dot(a9[...], slope_row[...]).astype(BF16)
    for b, y in enumerate(lane_shifted(hid_row[...].astype(F32))):
        for a in range(3):
            h9[48 * a + 16 * b : 48 * a + 16 * b + 16, :] = y[16 * a : 16 * a + 16]
    wsend[288:432, :] = dot(h9[...], cot_row[...]).astype(BF16)
    wsend[432:480, :] = jnp.zeros((48, 128), BF16)
    w_copy = remote(wsend.at[at(224 * (1 - core), 256, 32)], wcore, core_s.at[0], core_r.at[0], partner)
    w_copy.start()

    g_t[32:64, :] = dot_nt(u_ext[0:32, :], e_ref[...]).astype(BF16)
    g_t[16:32, :] = (dot_nt(qkv[0:16, :], d_ref[...]) * 0.25).astype(BF16)

    wait_all(feat_copies)
    turned = dot(g_t[...], featx[...])
    pblock[0:64, :] = turned[:, 0:128]
    pblock[64:128, :] = turned[:, 128:256]
    p2 = to_rows(0, lambda j: pblock.at[at(8 * j, 8, 8), :], lambda d: prow.at[d])
    w_copy.wait()
    whalf[...] = (wsend[at(224 * core, 256, 32), :].astype(F32) + wcore[...].astype(F32)).astype(BF16)
    w_copies = to_rows(1, lambda j: whalf.at[at(16 * j, 16, 16), :], lambda d: wrow.at[d])
    g_copies = to_cols(6, lambda j: g_t.at[:, at(128 * j, 128, 128)], lambda d: g_recv.at[at(64 * c, 64, 64), :])
    g_recv[at(64 * c, 64, 64), :] = g_t[:, my_lanes]

    wait_all(p2)
    total = pblock[at(8 * k, 8, 8), :]
    for d in range(1, 16):
        total = total + prow[d]
    pfin[...] = total
    p3 = remote(pfin, pcore, core_s.at[2], core_r.at[2], partner)
    p3.start()
    wait_all(w_copies)
    total = whalf[at(16 * k, 16, 16), :].astype(F32)
    for d in range(1, 16):
        total = total + wrow[d].astype(F32)
    wfin[...] = total.astype(BF16)
    wrgat[at(16 * k, 16, 16), :] = wfin[...]
    w_copies = to_rows(2, lambda j: wfin, lambda d: wrgat.at[at(16 * k, 16, 16), :])
    p3.wait()
    pmine[...] = pfin[...] + pcore[...]
    p4 = to_rows(3, lambda j: pmine, lambda d: prgat.at[at(8 * k, 8, 8), :])
    prgat[at(8 * k, 8, 8), :] = pmine[...]
    wait_all(w_copies)
    back = []
    for m in range(2):
        place = at(112 * c, 112, 16)
        wgat[core, m, place, :] = wrgat[112 * m : 112 * m + 112, :]
        back.append(to_cols(7 if m == 0 else 10, lambda j: wgat.at[core, m, place, :], lambda d: wgat.at[core, m, place, :]))
    wait_all(g_copies)
    parts = []
    for first, size in ((0, 16), (16, 16), (32, 32)):
        for h in range(8):
            parts.append(g_recv[64 * h + first : 64 * h + first + size, :].astype(F32))
    grads = jnp.transpose(jnp.concatenate(parts)).astype(BF16)
    ig_ref[...] = dot_nt(grads, proj[...]).astype(BF16)

    wait_all(p4)
    pgat[at(128 * c, 128, 128), :] = prgat[...].astype(BF16)
    block = pgat.at[at(128 * c, 128, 128), :]
    p5 = to_cols(9, lambda j: block, lambda d: block)
    swap = []
    for m in range(2):
        wait_all(back[m])
        cp = remote(wgat.at[core, m], wgat.at[core, m], core_s.at[3 + m], core_r.at[3 + m], partner)
        cp.start()
        swap.append(cp)
    wait_all(p5)
    for h in range(8):
        for side in range(2):
            base = 128 * h + 64 * side
            lanes = slice(128 * side, 128 * side + 128)
            p_out[16 * h : 16 * h + 16, lanes] = pgat[base : base + 16, :]
            p_out[128 + 16 * h : 144 + 16 * h, lanes] = pgat[base + 16 : base + 32, :]
            p_out[256 + 32 * h : 288 + 32 * h, lanes] = pgat[base + 32 : base + 64, :]
    for cp in swap:
        cp.wait()
    w_out[...] = wgat[...]


def finish_kernel(out_in, ig_in, w_in, p_in, out_ref, ig_ref, proj_ref, first_ref, second_ref):
    factor = 1.0 / math.sqrt(HEIGHT * WIDTH)
    out_ref[...] = out_in[...]
    ig_ref[...] = ig_in[...]
    proj_ref[...] = jnp.transpose(p_in[...].astype(F32)) * factor
    for h in range(8):
        for n in range(27):
            q, row = n // 7, 112 * h + 16 * (n % 7)
            values = w_in[q // 2, q % 2, row : row + 16, :].astype(F32) * factor
            if n < 18:
                start = 256 * (n // 2) + 32 * h + 16 * (n % 2)
                first_ref[start : start + 16, :] = values
            else:
                start = 128 * (n - 18) + 16 * h
                second_ref[start : start + 16, :] = values


def body(features, projection, first_kernel, second_kernel, cotangent):
    vm = pltpu.VMEM
    dma = pltpu.SemaphoreType.DMA
    out, grad, weights, proj_grad = pl.pallas_call(
        block_kernel,
        out_shape=(
            jax.ShapeDtypeStruct((128, 128), BF16),
            jax.ShapeDtypeStruct((128, 256), BF16),
            jax.ShapeDtypeStruct((2, 2, 896, 128), BF16),
            jax.ShapeDtypeStruct((512, 256), BF16),
        ),
        in_specs=[pl.BlockSpec(memory_space=pltpu.HBM)] * 5,
        out_specs=[pl.BlockSpec(memory_space=vm)] * 4,
        scratch_shapes=[
            vm((128, 256), BF16), vm((256, 512), BF16), vm((2304, 128), BF16), vm((1152, 128), BF16), vm((128, 128), BF16),
            vm((512, 128), BF16), vm((64, 1024), BF16), vm((32, 1024), BF16), vm((8, 1024), F32),
            vm((2, 1024, 256), F32), vm((1024, 1024), BF16), vm((1024, 1024), BF16),
            vm((1024, 16), BF16), vm((1024, 48), BF16), vm((48, 1024), BF16),
            vm((8, 32, 256), BF16), vm((256, 256), BF16), vm((5, 144, 256), BF16), vm((5, 144, 768), BF16),
            vm((16, 128), BF16), vm((16, 128), BF16), vm((5, 144, 128), BF16), vm((5, 144, 384), BF16),
            vm((3, 384, 128), BF16), vm((3, 384, 256), BF16), vm((3, 144, 128), F32),
            vm((3, 144, 384), BF16), vm((3, 144, 384), BF16),
            vm((256, 128), BF16), vm((32, 1024), BF16), vm((48, 1024), BF16),
            vm((64, 1024), BF16), vm((512, 128), BF16), vm((1024, 256), BF16),
            vm((2, 32, 1024), BF16), vm((128, 128), BF16), vm((1024, 128), BF16), vm((8, 48, 128), BF16),
            vm((48, 1024), BF16), vm((1024, 128), BF16), vm((288, 1024), BF16), vm((144, 1024), BF16),
            vm((480, 128), BF16), vm((256, 128), BF16), vm((256, 128), BF16), vm((16, 16, 128), BF16),
            vm((16, 128), BF16), vm((256, 128), BF16), vm((2, 2, 896, 128), BF16),
            vm((128, 128), F32), vm((16, 8, 128), F32), vm((8, 128), F32), vm((8, 128), F32),
            vm((128, 128), F32), vm((8, 128), F32), vm((1024, 128), BF16),
            dma((5,)), dma((5,)), dma((11, 8)), dma((11, 8)), dma((4, 16)), dma((4, 16)), dma((3, 4)), dma((3, 4)), dma((5,)),
        ],
        compiler_params=pltpu.CompilerParams(
            collective_id=0, has_side_effects=True, vmem_limit_bytes=32 * 1024 * 1024
        ),
    )(
        *(
            pltpu.with_memory_space_constraint(x, pltpu.HBM)
            for x in (
                features.reshape(128, 256),
                projection,
                first_kernel.reshape(2304, 128),
                second_kernel.reshape(1152, 128),
                cotangent.reshape(128, 128),
            )
        )
    )
    out, grad, proj_grad, first, second = pl.pallas_call(
        finish_kernel,
        out_shape=(
            jax.ShapeDtypeStruct((128, 128), BF16),
            jax.ShapeDtypeStruct((128, 256), BF16),
            jax.ShapeDtypeStruct((256, 512), F32),
            jax.ShapeDtypeStruct((2304, 128), F32),
            jax.ShapeDtypeStruct((1152, 128), F32),
        ),
        in_specs=[pl.BlockSpec(memory_space=vm)] * 4,
        out_specs=[pl.BlockSpec(memory_space=vm)] * 5,
        compiler_params=pltpu.CompilerParams(vmem_limit_bytes=16 * 1024 * 1024),
    )(out, grad, weights, proj_grad)
    return (
        out.reshape(1, 128, 128),
        grad.reshape(1, 128, 256),
        proj_grad,
        first.reshape(3, 3, 256, 128),
        second.reshape(3, 3, 128, 128),
    )


def solution(mesh):
    placed = (P("rows", "cols", None), P(), P(), P(), P("rows", "cols", None))
    return jax.shard_map(
        body,
        mesh=mesh,
        in_specs=placed,
        out_specs=(P("rows", "cols", None), P("rows", "cols", None), P(), P(), P()),
        check_vma=False,
    )
```

```python
import math

import jax
import jax.numpy as jnp
from jax import lax
from jax.experimental import pallas as pl
from jax.experimental.pallas import tpu as pltpu
from jax.sharding import PartitionSpec as P

MESH = pl.DeviceIdType.MESH
F32 = jnp.float32
BF16 = jnp.bfloat16
HEIGHT = 32
WIDTH = 1024


def remote(src, dst, send_sem, recv_sem, device):
    return pltpu.make_async_remote_copy(
        src_ref=src, dst_ref=dst, send_sem=send_sem, recv_sem=recv_sem,
        device_id=device, device_id_type=MESH,
    )


def at(start, size, align):
    return pl.ds(pl.multiple_of(start, align), size)


def dot(a, b):
    return jnp.dot(a, b, preferred_element_type=F32)


def dot_nt(a, b):
    return lax.dot_general(a, b, (((1,), (1,)), ((), ())), preferred_element_type=F32)


def dot_tn(a, b):
    return lax.dot_general(a, b, (((0,), (0,)), ((), ())), preferred_element_type=F32)


def shifted(x):
    return pltpu.roll(x, 1, 0), x, pltpu.roll(x, 143, 0)


def wait_all(copies):
    for cp in copies:
        cp.wait()


def block_kernel(
    feat_in, proj_in, k1_in, k2_in, cot_in, out_ref, ig_ref, w_out, p_out,
    feat, proj, k1, k2, cot,
    qkv_send, qkv, att_t, inv_ref, s_ref, e_ref, d_ref, kmat, vext, vext_t,
    att_send, att_recv, attx, imc, cot_l, cot_r, cotx, cim, k2t, k1t, tc,
    hx, sx, up_send, up_t, u_ext, g_t, g_recv, featx,
    att_near, slope_own, slope_row, hid_send, hid_row, cot_row, a9, h9,
    wsend, wcore, whalf, wrow, wfin, wrgat, wgat,
    pblock, prow, pfin, pcore, prgat, pmine, pgat,
    core_s, core_r, col_s, col_r, row_s, row_r, halo_s, halo_r, load_s,
):
    r = lax.axis_index("rows")
    c = lax.axis_index("cols")
    core = r % 2
    k = r // 2
    partner = (r + 1 - 2 * core, c)

    def col_dev(d):
        return (r, (c + d) % 8)

    def row_dev(d):
        return (2 * ((k + d) % 16) + core, c)

    def near(d):
        return ((r + d + 32) % 32, c)

    def to_cols(kind, src_of, dst):
        copies = []
        for d in range(1, 8):
            cp = remote(src_of((c + d) % 8), dst(d), col_s.at[kind, d], col_r.at[kind, d], col_dev(d))
            cp.start()
            copies.append(cp)
        return copies

    def to_rows(kind, src_of, dst):
        copies = []
        for d in range(1, 16):
            cp = remote(src_of((k + d) % 16), dst(d), row_s.at[kind, d], row_r.at[kind, d], row_dev(d))
            cp.start()
            copies.append(cp)
        return copies

    def to_near(kind, src, slots):
        copies = []
        for n, d in enumerate((-1, 1, -2, 2)):
            cp = remote(src, slots.at[2 - d], halo_s.at[kind, n], halo_r.at[kind, n], near(d))
            cp.start()
            copies.append(cp)
        return copies

    barrier = pltpu.get_barrier_semaphore()
    pl.semaphore_signal(barrier, inc=1, device_id=partner, device_id_type=MESH)
    pl.semaphore_signal(barrier, inc=1, device_id=near(2 * core - 1), device_id_type=MESH)
    for d in range(1, 8):
        pl.semaphore_signal(barrier, inc=1, device_id=col_dev(d), device_id_type=MESH)
    for d in range(1, 16):
        pl.semaphore_signal(barrier, inc=1, device_id=row_dev(d), device_id_type=MESH)

    loads = []
    for n, (src, dst) in enumerate(
        ((feat_in, feat), (proj_in, proj), (cot_in, cot), (k2_in, k2), (k1_in, k1))
    ):
        cp = pltpu.make_async_copy(src, dst, load_s.at[n])
        cp.start()
        loads.append(cp)

    wait_all(loads[0:2])
    packed = jnp.transpose(dot(feat[...], proj[...])).astype(BF16)
    for h in range(8):
        qkv_send[64 * h : 64 * h + 16, :] = packed[16 * h : 16 * h + 16]
        qkv_send[64 * h + 16 : 64 * h + 32, :] = packed[128 + 16 * h : 144 + 16 * h]
        qkv_send[64 * h + 32 : 64 * h + 64, :] = packed[256 + 32 * h : 288 + 32 * h]
    wait_all(loads[2:5])
    pl.semaphore_wait(barrier, 24)
    my_lanes = at(128 * c, 128, 128)
    qkv_copies = to_cols(
        0, lambda j: qkv_send.at[at(64 * j, 64, 64), :], lambda d: qkv.at[:, my_lanes]
    )
    left = remote(cot.at[112:128], cot_l, halo_s.at[2, 0], halo_r.at[2, 0], col_dev(1))
    left.start()
    right = remote(cot.at[0:16], cot_r, halo_s.at[2, 1], halo_r.at[2, 1], col_dev(7))
    right.start()
    qkv[:, my_lanes] = qkv_send[at(64 * c, 64, 64), :]
    for a in range(3):
        for b in range(3):
            n = 3 * a + b
            k2t[a, 128 * b : 128 * b + 128, :] = jnp.transpose(
                k2[128 * n : 128 * n + 128, :].astype(F32)
            ).astype(BF16)
            k1t[a, 128 * b : 128 * b + 128, :] = jnp.transpose(
                k1[256 * n : 256 * n + 256, :].astype(F32)
            ).astype(BF16)
    index = lax.broadcasted_iota(jnp.int32, (144, 128), 0)
    low_end = 136 - 8 * (c // 7)
    high_start = 136 + 8 * ((7 - c) // 7)

    def in_image(row):
        return jnp.where((row >= 0) & (row < HEIGHT), 1, 0)

    left.wait()
    right.wait()
    cotx[2] = jnp.where(
        (index < low_end) | (index >= high_start),
        jnp.concatenate([cot[...].astype(F32), cot_r[0:8, :].astype(F32), cot_l[8:16, :].astype(F32)]),
        0.0,
    ).astype(BF16)
    cot_copies = to_near(0, cotx.at[2], cotx)
    wait_all(qkv_copies)
    cot_row_copies = to_cols(8, lambda j: cot, lambda d: cot_row.at[at(128 * c, 128, 128), :])
    cot_row[at(128 * c, 128, 128), :] = cot[...]

    kmat[...] = (jnp.transpose(qkv[16:32, :].astype(F32)) * 0.25).astype(BF16)
    vext_t[0:32, :] = qkv[32:64, :]
    extra = lax.broadcasted_iota(jnp.int32, (16, 1024), 0)
    vext_t[32:48, :] = jnp.where(extra < 2, 1.0, 0.0).astype(BF16)
    vext[...] = jnp.transpose(vext_t[...].astype(F32)).astype(BF16)
    lane = lax.broadcasted_iota(jnp.int32, (32, 128), 1)
    zero = jnp.zeros((32, 128), F32)

    def send_attended(j):
        after = att_t[:, 128 * j + 128 : 128 * j + 256].astype(F32) if j < 7 else zero
        before = att_t[:, 128 * j - 128 : 128 * j].astype(F32) if j > 0 else zero
        att_send[j, :, 0:128] = att_t[:, 128 * j : 128 * j + 128]
        att_send[j, :, 128:256] = jnp.where(lane < 64, after, before).astype(BF16)

        @pl.when(c != j)
        def _():
            d = (j - c + 8) % 8
            remote(
                att_send.at[j], att_recv.at[at(32 * c, 32, 32), :], col_s.at[2, d], col_r.at[2, d], (r, j)
            ).start()

    def score(ib, jc, top):
        s = dot(kmat[128 * jc : 128 * jc + 128, :], qkv[0:16, 256 * ib : 256 * ib + 256])
        s_ref[ib % 2, 128 * jc : 128 * jc + 128, :] = s
        part = jnp.max(s.reshape(16, 8, 256), axis=0)
        return part if top is None else jnp.maximum(top, part)

    top_next = None
    for jc in range(8):
        top_next = score(0, jc, top_next)
    for ib in range(4):
        lanes = slice(256 * ib, 256 * ib + 256)
        top = jnp.max(top_next, axis=0, keepdims=True)
        top_next = None
        for jc in range(8):
            rows = slice(128 * jc, 128 * jc + 128)
            if ib < 3:
                top_next = score(ib + 1, jc, top_next)
            e_ref[rows, lanes] = jnp.exp(s_ref[ib % 2, rows, :] - top).astype(BF16)
        weighted = dot(vext_t[...], e_ref[:, lanes])
        inverse = 1.0 / weighted[32:33, :]
        inv_ref[0:1, lanes] = inverse
        att_t[:, lanes] = (weighted[0:32, :] * inverse).astype(BF16)
        for j in ((0,), (1, 2), (3, 4), (5, 6, 7))[ib]:
            send_attended(j)

    row_copies = []
    for n, d in enumerate((-1, 1)):
        cp = remote(att_t, att_near.at[n], halo_s.at[2, 2 + n], halo_r.at[2, 2 + n], near(d))
        cp.start()
        row_copies.append(cp)
    att_recv[at(32 * c, 32, 32), :] = att_send[c]

    wait_all(cot_copies)
    for slot in range(5):
        x = cotx[slot].astype(F32) * in_image(r - 2 + slot).astype(F32)
        low, mid, high = shifted(x)
        cim[slot, :, 0:128] = high.astype(BF16)
        cim[slot, :, 128:256] = mid.astype(BF16)
        cim[slot, :, 256:384] = low.astype(BF16)
    for t in range(3):
        tc[t] = (
            dot(cim[t + 2], k2t[0]) + dot(cim[t + 1], k2t[1]) + dot(cim[t], k2t[2])
        )

    for d in range(1, 8):
        remote(
            att_send.at[(c + d) % 8], att_recv.at[at(32 * c, 32, 32), :],
            col_s.at[2, d], col_r.at[2, d], col_dev(d),
        ).wait()
    turned = jnp.transpose(att_recv[...].astype(F32))
    attx[2] = jnp.concatenate([turned[0:136], turned[248:256]]).astype(BF16)
    near_copies = to_near(1, attx.at[2], attx)
    feat_copies = to_cols(1, lambda j: feat, lambda d: featx.at[at(128 * c, 128, 128), :])
    featx[at(128 * c, 128, 128), :] = feat[...]

    def columns(slot):
        x = attx[slot].astype(F32) * in_image(r - 2 + slot).astype(F32)
        low, mid, high = shifted(x)
        imc[slot, :, 0:256] = low.astype(BF16)
        imc[slot, :, 256:512] = mid.astype(BF16)
        imc[slot, :, 512:768] = high.astype(BF16)

    columns(2)
    column = lax.broadcasted_iota(jnp.int32, (48, 1024), 1)

    def lane_shifted(x):
        n = x.shape[0]
        low = jnp.where(column[0:n] == 0, 0.0, pltpu.roll(x, 1, 1))
        high = jnp.where(column[0:n] == 1023, 0.0, pltpu.roll(x, 1023, 1))
        return low.astype(BF16), x.astype(BF16), high.astype(BF16)

    wait_all(row_copies)
    for a in range(3):
        x = (att_near[1], att_t[...], att_near[0])[a].astype(F32) * in_image(r - 1 + a).astype(F32)
        for b, y in enumerate(lane_shifted(x)):
            a9[96 * a + 32 * b : 96 * a + 32 * b + 32, :] = y
    wait_all(near_copies[0:2])
    columns(1)
    columns(3)

    for t in (1, 0, 2):
        if t == 0:
            wait_all(near_copies[2:4])
            columns(0)
            columns(4)
        pre = (
            dot(imc[t], k1[0:768, :])
            + dot(imc[t + 1], k1[768:1536, :])
            + dot(imc[t + 2], k1[1536:2304, :])
        )
        valid = in_image(r - 1 + t)
        keep = (index < low_end * valid) | (index >= 144 - (144 - high_start) * valid)
        sigma = 1.0 / (1.0 + jnp.exp(-pre))
        slope = jnp.where(keep, tc[t] * (sigma * (1.0 + pre * (1.0 - sigma))), 0.0)
        low, mid, high = shifted(slope)
        sx[t, :, 0:128] = high.astype(BF16)
        sx[t, :, 128:256] = mid.astype(BF16)
        sx[t, :, 256:384] = low.astype(BF16)
        if t == 1:
            slope_own[...] = slope[0:128].astype(BF16)
            slope_copies = to_cols(4, lambda j: slope_own, lambda d: slope_row.at[at(128 * c, 128, 128), :])
        hidden = jnp.where(keep, pre * sigma, 0.0)
        low, mid, high = shifted(hidden)
        hx[t, :, 0:128] = low.astype(BF16)
        hx[t, :, 128:256] = mid.astype(BF16)
        hx[t, :, 256:384] = high.astype(BF16)

    upstream = (
        dot(sx[2, 0:128, :], k1t[0]) + dot(sx[1, 0:128, :], k1t[1]) + dot(sx[0, 0:128, :], k1t[2])
    )
    up_send[...] = jnp.transpose(upstream).astype(BF16)
    up_copies = to_cols(3, lambda j: up_send.at[at(32 * j, 32, 32), :], lambda d: up_t.at[:, my_lanes])
    up_t[:, my_lanes] = up_send[at(32 * c, 32, 32), :]

    for t in range(3):
        turned = jnp.transpose(hx[t, 0:128, 128:256].astype(F32)).astype(BF16)
        for j in range(8):
            hid_send[j, 16 * t : 16 * t + 16, :] = turned[16 * j : 16 * j + 16]
    hid_copies = to_cols(5, lambda j: hid_send.at[j], lambda d: hid_row.at[:, my_lanes])
    slope_row[at(128 * c, 128, 128), :] = slope_own[...]
    hid_row[:, my_lanes] = hid_send[c]
    out_ref[...] = (
        dot(hx[0, 0:128, :], k2[0:384, :])
        + dot(hx[1, 0:128, :], k2[384:768, :])
        + dot(hx[2, 0:128, :], k2[768:1152, :])
    ).astype(BF16)

    wait_all(up_copies)
    scaled = (up_t[...].astype(F32) * inv_ref[0:1, :]).astype(BF16)
    u_ext[0:32, :] = scaled
    inner = jnp.sum(scaled.astype(F32) * att_t[...].astype(F32), axis=0, keepdims=True)
    inner_high = inner.astype(BF16).astype(F32)
    extra = lax.broadcasted_iota(jnp.int32, (16, 1024), 0)
    u_ext[32:48, :] = jnp.where(
        extra == 0, -inner_high, jnp.where(extra == 1, inner_high - inner, 0.0)
    ).astype(BF16)

    def backward(ib):
        lanes = slice(256 * ib, 256 * ib + 256)
        u_block = u_ext[:, lanes]
        for jc in range(8):
            rows = slice(128 * jc, 128 * jc + 128)
            slopes = dot(vext[rows, :], u_block)
            d_ref[rows, lanes] = (e_ref[rows, lanes].astype(F32) * slopes).astype(BF16)
        g_t[0:16, lanes] = (dot(qkv[16:32, :], d_ref[:, lanes]) * 0.25).astype(BF16)

    backward(0)
    backward(1)
    backward(2)
    backward(3)

    wait_all(slope_copies)
    wait_all(cot_row_copies)
    wait_all(hid_copies)
    wsend[0:288, :] = dot(a9[...], slope_row[...]).astype(BF16)
    for b, y in enumerate(lane_shifted(hid_row[...].astype(F32))):
        for a in range(3):
            h9[48 * a + 16 * b : 48 * a + 16 * b + 16, :] = y[16 * a : 16 * a + 16]
    wsend[288:432, :] = dot(h9[...], cot_row[...]).astype(BF16)
    wsend[432:480, :] = jnp.zeros((48, 128), BF16)
    w_copy = remote(wsend.at[at(224 * (1 - core), 256, 32)], wcore, core_s.at[0], core_r.at[0], partner)
    w_copy.start()

    g_t[32:64, :] = dot_nt(u_ext[0:32, :], e_ref[...]).astype(BF16)
    g_t[16:32, :] = (dot_nt(qkv[0:16, :], d_ref[...]) * 0.25).astype(BF16)

    wait_all(feat_copies)
    turned = dot(g_t[...], featx[...])
    pblock[0:64, :] = turned[:, 0:128]
    pblock[64:128, :] = turned[:, 128:256]
    p2 = to_rows(0, lambda j: pblock.at[at(8 * j, 8, 8), :], lambda d: prow.at[d])
    w_copy.wait()
    whalf[...] = (wsend[at(224 * core, 256, 32), :].astype(F32) + wcore[...].astype(F32)).astype(BF16)
    w_copies = to_rows(1, lambda j: whalf.at[at(16 * j, 16, 16), :], lambda d: wrow.at[d])
    g_copies = to_cols(6, lambda j: g_t.at[:, at(128 * j, 128, 128)], lambda d: g_recv.at[at(64 * c, 64, 64), :])
    g_recv[at(64 * c, 64, 64), :] = g_t[:, my_lanes]

    wait_all(p2)
    total = pblock[at(8 * k, 8, 8), :]
    for d in range(1, 16):
        total = total + prow[d]
    pfin[...] = total
    p3 = remote(pfin, pcore, core_s.at[2], core_r.at[2], partner)
    p3.start()
    wait_all(w_copies)
    total = whalf[at(16 * k, 16, 16), :].astype(F32)
    for d in range(1, 16):
        total = total + wrow[d].astype(F32)
    wfin[...] = total.astype(BF16)
    wrgat[at(16 * k, 16, 16), :] = wfin[...]
    w_copies = to_rows(2, lambda j: wfin, lambda d: wrgat.at[at(16 * k, 16, 16), :])
    p3.wait()
    pmine[...] = pfin[...] + pcore[...]
    p4 = to_rows(3, lambda j: pmine, lambda d: prgat.at[at(8 * k, 8, 8), :])
    prgat[at(8 * k, 8, 8), :] = pmine[...]
    wait_all(w_copies)
    back = []
    for m in range(2):
        place = at(112 * c, 112, 16)
        wgat[core, m, place, :] = wrgat[112 * m : 112 * m + 112, :]
        back.append(to_cols(7 if m == 0 else 10, lambda j: wgat.at[core, m, place, :], lambda d: wgat.at[core, m, place, :]))
    wait_all(g_copies)
    parts = []
    for first, size in ((0, 16), (16, 16), (32, 32)):
        for h in range(8):
            parts.append(g_recv[64 * h + first : 64 * h + first + size, :].astype(F32))
    grads = jnp.transpose(jnp.concatenate(parts)).astype(BF16)
    ig_ref[...] = dot_nt(grads, proj[...]).astype(BF16)

    wait_all(p4)
    pgat[at(128 * c, 128, 128), :] = prgat[...].astype(BF16)
    block = pgat.at[at(128 * c, 128, 128), :]
    p5 = to_cols(9, lambda j: block, lambda d: block)
    swap = []
    for m in range(2):
        wait_all(back[m])
        cp = remote(wgat.at[core, m], wgat.at[core, m], core_s.at[3 + m], core_r.at[3 + m], partner)
        cp.start()
        swap.append(cp)
    wait_all(p5)
    for h in range(8):
        for side in range(2):
            base = 128 * h + 64 * side
            lanes = slice(128 * side, 128 * side + 128)
            p_out[16 * h : 16 * h + 16, lanes] = pgat[base : base + 16, :]
            p_out[128 + 16 * h : 144 + 16 * h, lanes] = pgat[base + 16 : base + 32, :]
            p_out[256 + 32 * h : 288 + 32 * h, lanes] = pgat[base + 32 : base + 64, :]
    for cp in swap:
        cp.wait()
    w_out[...] = wgat[...]


def finish_kernel(out_in, ig_in, w_in, p_in, out_ref, ig_ref, proj_ref, first_ref, second_ref):
    factor = 1.0 / math.sqrt(HEIGHT * WIDTH)
    out_ref[...] = out_in[...]
    ig_ref[...] = ig_in[...]
    proj_ref[...] = jnp.transpose(p_in[...].astype(F32)) * factor
    for h in range(8):
        for n in range(27):
            q, row = n // 7, 112 * h + 16 * (n % 7)
            values = w_in[q // 2, q % 2, row : row + 16, :].astype(F32) * factor
            if n < 18:
                start = 256 * (n // 2) + 32 * h + 16 * (n % 2)
                first_ref[start : start + 16, :] = values
            else:
                start = 128 * (n - 18) + 16 * h
                second_ref[start : start + 16, :] = values


def body(features, projection, first_kernel, second_kernel, cotangent):
    vm = pltpu.VMEM
    dma = pltpu.SemaphoreType.DMA
    out, grad, weights, proj_grad = pl.pallas_call(
        block_kernel,
        out_shape=(
            jax.ShapeDtypeStruct((128, 128), BF16),
            jax.ShapeDtypeStruct((128, 256), BF16),
            jax.ShapeDtypeStruct((2, 2, 896, 128), BF16),
            jax.ShapeDtypeStruct((512, 256), BF16),
        ),
        in_specs=[pl.BlockSpec(memory_space=pltpu.HBM)] * 5,
        out_specs=[pl.BlockSpec(memory_space=vm)] * 4,
        scratch_shapes=[
            vm((128, 256), BF16), vm((256, 512), BF16), vm((2304, 128), BF16), vm((1152, 128), BF16), vm((128, 128), BF16),
            vm((512, 128), BF16), vm((64, 1024), BF16), vm((32, 1024), BF16), vm((8, 1024), F32),
            vm((2, 1024, 256), F32), vm((1024, 1024), BF16), vm((1024, 1024), BF16),
            vm((1024, 16), BF16), vm((1024, 48), BF16), vm((48, 1024), BF16),
            vm((8, 32, 256), BF16), vm((256, 256), BF16), vm((5, 144, 256), BF16), vm((5, 144, 768), BF16),
            vm((16, 128), BF16), vm((16, 128), BF16), vm((5, 144, 128), BF16), vm((5, 144, 384), BF16),
            vm((3, 384, 128), BF16), vm((3, 384, 256), BF16), vm((3, 144, 128), F32),
            vm((3, 144, 384), BF16), vm((3, 144, 384), BF16),
            vm((256, 128), BF16), vm((32, 1024), BF16), vm((48, 1024), BF16),
            vm((64, 1024), BF16), vm((512, 128), BF16), vm((1024, 256), BF16),
            vm((2, 32, 1024), BF16), vm((128, 128), BF16), vm((1024, 128), BF16), vm((8, 48, 128), BF16),
            vm((48, 1024), BF16), vm((1024, 128), BF16), vm((288, 1024), BF16), vm((144, 1024), BF16),
            vm((480, 128), BF16), vm((256, 128), BF16), vm((256, 128), BF16), vm((16, 16, 128), BF16),
            vm((16, 128), BF16), vm((256, 128), BF16), vm((2, 2, 896, 128), BF16),
            vm((128, 128), F32), vm((16, 8, 128), F32), vm((8, 128), F32), vm((8, 128), F32),
            vm((128, 128), F32), vm((8, 128), F32), vm((1024, 128), BF16),
            dma((5,)), dma((5,)), dma((11, 8)), dma((11, 8)), dma((4, 16)), dma((4, 16)), dma((3, 4)), dma((3, 4)), dma((5,)),
        ],
        compiler_params=pltpu.CompilerParams(
            collective_id=0, has_side_effects=True, vmem_limit_bytes=32 * 1024 * 1024
        ),
    )(
        *(
            pltpu.with_memory_space_constraint(x, pltpu.HBM)
            for x in (
                features.reshape(128, 256),
                projection,
                first_kernel.reshape(2304, 128),
                second_kernel.reshape(1152, 128),
                cotangent.reshape(128, 128),
            )
        )
    )
    out, grad, proj_grad, first, second = pl.pallas_call(
        finish_kernel,
        out_shape=(
            jax.ShapeDtypeStruct((128, 128), BF16),
            jax.ShapeDtypeStruct((128, 256), BF16),
            jax.ShapeDtypeStruct((256, 512), F32),
            jax.ShapeDtypeStruct((2304, 128), F32),
            jax.ShapeDtypeStruct((1152, 128), F32),
        ),
        in_specs=[pl.BlockSpec(memory_space=vm)] * 4,
        out_specs=[pl.BlockSpec(memory_space=vm)] * 5,
        compiler_params=pltpu.CompilerParams(vmem_limit_bytes=16 * 1024 * 1024),
    )(out, grad, weights, proj_grad)
    return (
        out.reshape(1, 128, 128),
        grad.reshape(1, 128, 256),
        proj_grad,
        first.reshape(3, 3, 256, 128),
        second.reshape(3, 3, 128, 128),
    )


def solution(mesh):
    placed = (P("rows", "cols", None), P(), P(), P(), P("rows", "cols", None))
    return jax.shard_map(
        body,
        mesh=mesh,
        in_specs=placed,
        out_specs=(P("rows", "cols", None), P("rows", "cols", None), P(), P(), P()),
        check_vma=False,
    )
```

```python
import math

import jax
import jax.numpy as jnp
from jax import lax
from jax.experimental import pallas as pl
from jax.experimental.pallas import tpu as pltpu
from jax.sharding import PartitionSpec as P

MESH = pl.DeviceIdType.MESH
F32 = jnp.float32
BF16 = jnp.bfloat16
HEIGHT = 32
WIDTH = 1024


def remote(src, dst, send_sem, recv_sem, device):
    return pltpu.make_async_remote_copy(
        src_ref=src, dst_ref=dst, send_sem=send_sem, recv_sem=recv_sem,
        device_id=device, device_id_type=MESH,
    )


def at(start, size, align):
    return pl.ds(pl.multiple_of(start, align), size)


def dot(a, b):
    return jnp.dot(a, b, preferred_element_type=F32)


def dot_nt(a, b):
    return lax.dot_general(a, b, (((1,), (1,)), ((), ())), preferred_element_type=F32)


def dot_tn(a, b):
    return lax.dot_general(a, b, (((0,), (0,)), ((), ())), preferred_element_type=F32)


def shifted(x):
    return pltpu.roll(x, 1, 0), x, pltpu.roll(x, 143, 0)


def wait_all(copies):
    for cp in copies:
        cp.wait()


def block_kernel(
    feat_in, proj_in, k1_in, k2_in, cot_in, out_ref, ig_ref, w_out, p_out,
    feat, proj, k1, k2, cot,
    qkv_send, qkv, att_t, inv_ref, s_ref, e_ref, d_ref, kmat, vext, vext_t,
    att_send, att_recv, attx, imc, cot_l, cot_r, cotx, cim, k2t, k1t, tc,
    hx, sx, up_send, up_t, u_ext, g_t, g_recv, featx,
    att_near, slope_own, slope_row, hid_send, hid_row, cot_row, a9, h9,
    wsend, wcore, whalf, wrow, wfin, wrgat, wgat,
    pblock, prow, pfin, pcore, prgat, pmine, pgat,
    core_s, core_r, col_s, col_r, row_s, row_r, halo_s, halo_r, load_s,
):
    r = lax.axis_index("rows")
    c = lax.axis_index("cols")
    core = r % 2
    k = r // 2
    partner = (r + 1 - 2 * core, c)

    def col_dev(d):
        return (r, (c + d) % 8)

    def row_dev(d):
        return (2 * ((k + d) % 16) + core, c)

    def near(d):
        return ((r + d + 32) % 32, c)

    def to_cols(kind, src_of, dst):
        copies = []
        for d in range(1, 8):
            cp = remote(src_of((c + d) % 8), dst(d), col_s.at[kind, d], col_r.at[kind, d], col_dev(d))
            cp.start()
            copies.append(cp)
        return copies

    def to_rows(kind, src_of, dst):
        copies = []
        for d in range(1, 16):
            cp = remote(src_of((k + d) % 16), dst(d), row_s.at[kind, d], row_r.at[kind, d], row_dev(d))
            cp.start()
            copies.append(cp)
        return copies

    def to_near(kind, src, slots):
        copies = []
        for n, d in enumerate((-1, 1, -2, 2)):
            cp = remote(src, slots.at[2 - d], halo_s.at[kind, n], halo_r.at[kind, n], near(d))
            cp.start()
            copies.append(cp)
        return copies

    barrier = pltpu.get_barrier_semaphore()
    pl.semaphore_signal(barrier, inc=1, device_id=partner, device_id_type=MESH)
    pl.semaphore_signal(barrier, inc=1, device_id=near(2 * core - 1), device_id_type=MESH)
    for d in range(1, 8):
        pl.semaphore_signal(barrier, inc=1, device_id=col_dev(d), device_id_type=MESH)
    for d in range(1, 16):
        pl.semaphore_signal(barrier, inc=1, device_id=row_dev(d), device_id_type=MESH)

    loads = []
    for n, (src, dst) in enumerate(
        ((feat_in, feat), (proj_in, proj), (cot_in, cot), (k2_in, k2), (k1_in, k1))
    ):
        cp = pltpu.make_async_copy(src, dst, load_s.at[n])
        cp.start()
        loads.append(cp)

    wait_all(loads[0:2])
    packed = jnp.transpose(dot(feat[...], proj[...])).astype(BF16)
    for h in range(8):
        qkv_send[64 * h : 64 * h + 16, :] = packed[16 * h : 16 * h + 16]
        qkv_send[64 * h + 16 : 64 * h + 32, :] = packed[128 + 16 * h : 144 + 16 * h]
        qkv_send[64 * h + 32 : 64 * h + 64, :] = packed[256 + 32 * h : 288 + 32 * h]
    wait_all(loads[2:5])
    pl.semaphore_wait(barrier, 24)
    my_lanes = at(128 * c, 128, 128)
    qkv_copies = to_cols(
        0, lambda j: qkv_send.at[at(64 * j, 64, 64), :], lambda d: qkv.at[:, my_lanes]
    )
    left = remote(cot.at[112:128], cot_l, halo_s.at[2, 0], halo_r.at[2, 0], col_dev(1))
    left.start()
    right = remote(cot.at[0:16], cot_r, halo_s.at[2, 1], halo_r.at[2, 1], col_dev(7))
    right.start()
    qkv[:, my_lanes] = qkv_send[at(64 * c, 64, 64), :]
    for a in range(3):
        for b in range(3):
            n = 3 * a + b
            k2t[a, 128 * b : 128 * b + 128, :] = jnp.transpose(
                k2[128 * n : 128 * n + 128, :].astype(F32)
            ).astype(BF16)
            k1t[a, 128 * b : 128 * b + 128, :] = jnp.transpose(
                k1[256 * n : 256 * n + 256, :].astype(F32)
            ).astype(BF16)
    index = lax.broadcasted_iota(jnp.int32, (144, 128), 0)
    low_end = 136 - 8 * (c // 7)
    high_start = 136 + 8 * ((7 - c) // 7)

    def in_image(row):
        return jnp.where((row >= 0) & (row < HEIGHT), 1, 0)

    left.wait()
    right.wait()
    cotx[2] = jnp.where(
        (index < low_end) | (index >= high_start),
        jnp.concatenate([cot[...].astype(F32), cot_r[0:8, :].astype(F32), cot_l[8:16, :].astype(F32)]),
        0.0,
    ).astype(BF16)
    cot_copies = to_near(0, cotx.at[2], cotx)
    wait_all(qkv_copies)
    cot_row_copies = to_cols(8, lambda j: cot, lambda d: cot_row.at[at(128 * c, 128, 128), :])
    cot_row[at(128 * c, 128, 128), :] = cot[...]

    kmat[...] = (jnp.transpose(qkv[16:32, :].astype(F32)) * 0.25).astype(BF16)
    vext_t[0:32, :] = qkv[32:64, :]
    extra = lax.broadcasted_iota(jnp.int32, (16, 1024), 0)
    vext_t[32:48, :] = jnp.where(extra < 2, 1.0, 0.0).astype(BF16)
    vext[...] = jnp.transpose(vext_t[...].astype(F32)).astype(BF16)
    lane = lax.broadcasted_iota(jnp.int32, (32, 128), 1)
    zero = jnp.zeros((32, 128), F32)

    def send_attended(j):
        after = att_t[:, 128 * j + 128 : 128 * j + 256].astype(F32) if j < 7 else zero
        before = att_t[:, 128 * j - 128 : 128 * j].astype(F32) if j > 0 else zero
        att_send[j, :, 0:128] = att_t[:, 128 * j : 128 * j + 128]
        att_send[j, :, 128:256] = jnp.where(lane < 64, after, before).astype(BF16)

        @pl.when(c != j)
        def _():
            d = (j - c + 8) % 8
            remote(
                att_send.at[j], att_recv.at[at(32 * c, 32, 32), :], col_s.at[2, d], col_r.at[2, d], (r, j)
            ).start()

    def score(ib, jc, top):
        s = dot(kmat[128 * jc : 128 * jc + 128, :], qkv[0:16, 256 * ib : 256 * ib + 256])
        s_ref[ib % 2, 128 * jc : 128 * jc + 128, :] = s
        part = jnp.max(s.reshape(16, 8, 256), axis=0)
        return part if top is None else jnp.maximum(top, part)

    top_next = None
    for jc in range(8):
        top_next = score(0, jc, top_next)
    for ib in range(4):
        lanes = slice(256 * ib, 256 * ib + 256)
        top = jnp.max(top_next, axis=0, keepdims=True)
        top_next = None
        for jc in range(8):
            rows = slice(128 * jc, 128 * jc + 128)
            if ib < 3:
                top_next = score(ib + 1, jc, top_next)
            e_ref[rows, lanes] = jnp.exp(s_ref[ib % 2, rows, :] - top).astype(BF16)
        weighted = dot(vext_t[...], e_ref[:, lanes])
        inverse = 1.0 / weighted[32:33, :]
        inv_ref[0:1, lanes] = inverse
        att_t[:, lanes] = (weighted[0:32, :] * inverse).astype(BF16)
        for j in ((0,), (1, 2), (3, 4), (5, 6, 7))[ib]:
            send_attended(j)

    row_copies = []
    for n, d in enumerate((-1, 1)):
        cp = remote(att_t, att_near.at[n], halo_s.at[2, 2 + n], halo_r.at[2, 2 + n], near(d))
        cp.start()
        row_copies.append(cp)
    att_recv[at(32 * c, 32, 32), :] = att_send[c]

    wait_all(cot_copies)
    for slot in range(5):
        x = cotx[slot].astype(F32) * in_image(r - 2 + slot).astype(F32)
        low, mid, high = shifted(x)
        cim[slot, :, 0:128] = high.astype(BF16)
        cim[slot, :, 128:256] = mid.astype(BF16)
        cim[slot, :, 256:384] = low.astype(BF16)
    for t in range(3):
        tc[t] = (
            dot(cim[t + 2], k2t[0]) + dot(cim[t + 1], k2t[1]) + dot(cim[t], k2t[2])
        )

    for d in range(1, 8):
        remote(
            att_send.at[(c + d) % 8], att_recv.at[at(32 * c, 32, 32), :],
            col_s.at[2, d], col_r.at[2, d], col_dev(d),
        ).wait()
    turned = jnp.transpose(att_recv[...].astype(F32))
    attx[2] = jnp.concatenate([turned[0:136], turned[248:256]]).astype(BF16)
    near_copies = to_near(1, attx.at[2], attx)

    def columns(slot):
        x = attx[slot].astype(F32) * in_image(r - 2 + slot).astype(F32)
        low, mid, high = shifted(x)
        imc[slot, :, 0:256] = low.astype(BF16)
        imc[slot, :, 256:512] = mid.astype(BF16)
        imc[slot, :, 512:768] = high.astype(BF16)

    columns(2)
    column = lax.broadcasted_iota(jnp.int32, (48, 1024), 1)

    def lane_shifted(x):
        n = x.shape[0]
        low = jnp.where(column[0:n] == 0, 0.0, pltpu.roll(x, 1, 1))
        high = jnp.where(column[0:n] == 1023, 0.0, pltpu.roll(x, 1023, 1))
        return low.astype(BF16), x.astype(BF16), high.astype(BF16)

    wait_all(row_copies)
    for a in range(3):
        x = (att_near[1], att_t[...], att_near[0])[a].astype(F32) * in_image(r - 1 + a).astype(F32)
        for b, y in enumerate(lane_shifted(x)):
            a9[96 * a + 32 * b : 96 * a + 32 * b + 32, :] = y
    wait_all(near_copies[0:2])
    columns(1)
    columns(3)

    for t in (1, 0, 2):
        if t == 0:
            wait_all(near_copies[2:4])
            columns(0)
            columns(4)
        pre = (
            dot(imc[t], k1[0:768, :])
            + dot(imc[t + 1], k1[768:1536, :])
            + dot(imc[t + 2], k1[1536:2304, :])
        )
        valid = in_image(r - 1 + t)
        keep = (index < low_end * valid) | (index >= 144 - (144 - high_start) * valid)
        sigma = 1.0 / (1.0 + jnp.exp(-pre))
        slope = jnp.where(keep, tc[t] * (sigma * (1.0 + pre * (1.0 - sigma))), 0.0)
        low, mid, high = shifted(slope)
        sx[t, :, 0:128] = high.astype(BF16)
        sx[t, :, 128:256] = mid.astype(BF16)
        sx[t, :, 256:384] = low.astype(BF16)
        if t == 1:
            slope_own[...] = slope[0:128].astype(BF16)
            slope_copies = to_cols(4, lambda j: slope_own, lambda d: slope_row.at[at(128 * c, 128, 128), :])
        hidden = jnp.where(keep, pre * sigma, 0.0)
        low, mid, high = shifted(hidden)
        hx[t, :, 0:128] = low.astype(BF16)
        hx[t, :, 128:256] = mid.astype(BF16)
        hx[t, :, 256:384] = high.astype(BF16)

    upstream = (
        dot(sx[2, 0:128, :], k1t[0]) + dot(sx[1, 0:128, :], k1t[1]) + dot(sx[0, 0:128, :], k1t[2])
    )
    up_send[...] = jnp.transpose(upstream).astype(BF16)
    up_copies = to_cols(3, lambda j: up_send.at[at(32 * j, 32, 32), :], lambda d: up_t.at[:, my_lanes])
    up_t[:, my_lanes] = up_send[at(32 * c, 32, 32), :]

    for t in range(3):
        turned = jnp.transpose(hx[t, 0:128, 128:256].astype(F32)).astype(BF16)
        for j in range(8):
            hid_send[j, 16 * t : 16 * t + 16, :] = turned[16 * j : 16 * j + 16]
    hid_copies = to_cols(5, lambda j: hid_send.at[j], lambda d: hid_row.at[:, my_lanes])
    feat_copies = to_cols(1, lambda j: feat, lambda d: featx.at[at(128 * c, 128, 128), :])
    featx[at(128 * c, 128, 128), :] = feat[...]
    slope_row[at(128 * c, 128, 128), :] = slope_own[...]
    hid_row[:, my_lanes] = hid_send[c]
    out_ref[...] = (
        dot(hx[0, 0:128, :], k2[0:384, :])
        + dot(hx[1, 0:128, :], k2[384:768, :])
        + dot(hx[2, 0:128, :], k2[768:1152, :])
    ).astype(BF16)

    wait_all(up_copies)
    scaled = (up_t[...].astype(F32) * inv_ref[0:1, :]).astype(BF16)
    u_ext[0:32, :] = scaled
    inner = jnp.sum(scaled.astype(F32) * att_t[...].astype(F32), axis=0, keepdims=True)
    inner_high = inner.astype(BF16).astype(F32)
    extra = lax.broadcasted_iota(jnp.int32, (16, 1024), 0)
    u_ext[32:48, :] = jnp.where(
        extra == 0, -inner_high, jnp.where(extra == 1, inner_high - inner, 0.0)
    ).astype(BF16)

    def backward(ib):
        lanes = slice(256 * ib, 256 * ib + 256)
        u_block = u_ext[:, lanes]
        for jc in range(8):
            rows = slice(128 * jc, 128 * jc + 128)
            slopes = dot(vext[rows, :], u_block)
            d_ref[rows, lanes] = (e_ref[rows, lanes].astype(F32) * slopes).astype(BF16)
        g_t[0:16, lanes] = (dot(qkv[16:32, :], d_ref[:, lanes]) * 0.25).astype(BF16)

    backward(0)
    backward(1)
    backward(2)
    backward(3)

    wait_all(slope_copies)
    wait_all(cot_row_copies)
    wait_all(hid_copies)
    wsend[0:288, :] = dot(a9[...], slope_row[...]).astype(BF16)
    for b, y in enumerate(lane_shifted(hid_row[...].astype(F32))):
        for a in range(3):
            h9[48 * a + 16 * b : 48 * a + 16 * b + 16, :] = y[16 * a : 16 * a + 16]
    wsend[288:432, :] = dot(h9[...], cot_row[...]).astype(BF16)
    wsend[432:480, :] = jnp.zeros((48, 128), BF16)
    w_copy = remote(wsend.at[at(224 * (1 - core), 256, 32)], wcore, core_s.at[0], core_r.at[0], partner)
    w_copy.start()

    g_t[32:64, :] = dot_nt(u_ext[0:32, :], e_ref[...]).astype(BF16)
    g_t[16:32, :] = (dot_nt(qkv[0:16, :], d_ref[...]) * 0.25).astype(BF16)

    w_copy.wait()
    whalf[...] = (wsend[at(224 * core, 256, 32), :].astype(F32) + wcore[...].astype(F32)).astype(BF16)
    w_copies = to_rows(1, lambda j: whalf.at[at(16 * j, 16, 16), :], lambda d: wrow.at[d])

    wait_all(feat_copies)
    turned = dot(g_t[...], featx[...])
    pblock[0:64, :] = turned[:, 0:128]
    pblock[64:128, :] = turned[:, 128:256]
    p2 = to_rows(0, lambda j: pblock.at[at(8 * j, 8, 8), :], lambda d: prow.at[d])
    g_copies = to_cols(6, lambda j: g_t.at[:, at(128 * j, 128, 128)], lambda d: g_recv.at[at(64 * c, 64, 64), :])
    g_recv[at(64 * c, 64, 64), :] = g_t[:, my_lanes]

    wait_all(p2)
    total = pblock[at(8 * k, 8, 8), :]
    for d in range(1, 16):
        total = total + prow[d]
    pfin[...] = total
    p3 = remote(pfin, pcore, core_s.at[2], core_r.at[2], partner)
    p3.start()
    wait_all(w_copies)
    total = whalf[at(16 * k, 16, 16), :].astype(F32)
    for d in range(1, 16):
        total = total + wrow[d].astype(F32)
    wfin[...] = total.astype(BF16)
    wrgat[at(16 * k, 16, 16), :] = wfin[...]
    w_copies = to_rows(2, lambda j: wfin, lambda d: wrgat.at[at(16 * k, 16, 16), :])
    p3.wait()
    pmine[...] = pfin[...] + pcore[...]
    p4 = to_rows(3, lambda j: pmine, lambda d: prgat.at[at(8 * k, 8, 8), :])
    prgat[at(8 * k, 8, 8), :] = pmine[...]
    wait_all(w_copies)
    back = []
    for m in range(2):
        place = at(112 * c, 112, 16)
        wgat[core, m, place, :] = wrgat[112 * m : 112 * m + 112, :]
        back.append(to_cols(7 if m == 0 else 10, lambda j: wgat.at[core, m, place, :], lambda d: wgat.at[core, m, place, :]))
    wait_all(g_copies)
    parts = []
    for first, size in ((0, 16), (16, 16), (32, 32)):
        for h in range(8):
            parts.append(g_recv[64 * h + first : 64 * h + first + size, :].astype(F32))
    grads = jnp.transpose(jnp.concatenate(parts)).astype(BF16)
    ig_ref[...] = dot_nt(grads, proj[...]).astype(BF16)

    wait_all(p4)
    pgat[at(128 * c, 128, 128), :] = prgat[...].astype(BF16)
    block = pgat.at[at(128 * c, 128, 128), :]
    p5 = to_cols(9, lambda j: block, lambda d: block)
    swap = []
    for m in range(2):
        wait_all(back[m])
        cp = remote(wgat.at[core, m], wgat.at[core, m], core_s.at[3 + m], core_r.at[3 + m], partner)
        cp.start()
        swap.append(cp)
    wait_all(p5)
    for h in range(8):
        for side in range(2):
            base = 128 * h + 64 * side
            lanes = slice(128 * side, 128 * side + 128)
            p_out[16 * h : 16 * h + 16, lanes] = pgat[base : base + 16, :]
            p_out[128 + 16 * h : 144 + 16 * h, lanes] = pgat[base + 16 : base + 32, :]
            p_out[256 + 32 * h : 288 + 32 * h, lanes] = pgat[base + 32 : base + 64, :]
    for cp in swap:
        cp.wait()
    w_out[...] = wgat[...]


def finish_kernel(out_in, ig_in, w_in, p_in, out_ref, ig_ref, proj_ref, first_ref, second_ref):
    factor = 1.0 / math.sqrt(HEIGHT * WIDTH)
    out_ref[...] = out_in[...]
    ig_ref[...] = ig_in[...]
    proj_ref[...] = jnp.transpose(p_in[...].astype(F32)) * factor
    for h in range(8):
        for n in range(27):
            q, row = n // 7, 112 * h + 16 * (n % 7)
            values = w_in[q // 2, q % 2, row : row + 16, :].astype(F32) * factor
            if n < 18:
                start = 256 * (n // 2) + 32 * h + 16 * (n % 2)
                first_ref[start : start + 16, :] = values
            else:
                start = 128 * (n - 18) + 16 * h
                second_ref[start : start + 16, :] = values


def body(features, projection, first_kernel, second_kernel, cotangent):
    vm = pltpu.VMEM
    dma = pltpu.SemaphoreType.DMA
    out, grad, weights, proj_grad = pl.pallas_call(
        block_kernel,
        out_shape=(
            jax.ShapeDtypeStruct((128, 128), BF16),
            jax.ShapeDtypeStruct((128, 256), BF16),
            jax.ShapeDtypeStruct((2, 2, 896, 128), BF16),
            jax.ShapeDtypeStruct((512, 256), BF16),
        ),
        in_specs=[pl.BlockSpec(memory_space=pltpu.HBM)] * 5,
        out_specs=[pl.BlockSpec(memory_space=vm)] * 4,
        scratch_shapes=[
            vm((128, 256), BF16), vm((256, 512), BF16), vm((2304, 128), BF16), vm((1152, 128), BF16), vm((128, 128), BF16),
            vm((512, 128), BF16), vm((64, 1024), BF16), vm((32, 1024), BF16), vm((8, 1024), F32),
            vm((2, 1024, 256), F32), vm((1024, 1024), BF16), vm((1024, 1024), BF16),
            vm((1024, 16), BF16), vm((1024, 48), BF16), vm((48, 1024), BF16),
            vm((8, 32, 256), BF16), vm((256, 256), BF16), vm((5, 144, 256), BF16), vm((5, 144, 768), BF16),
            vm((16, 128), BF16), vm((16, 128), BF16), vm((5, 144, 128), BF16), vm((5, 144, 384), BF16),
            vm((3, 384, 128), BF16), vm((3, 384, 256), BF16), vm((3, 144, 128), F32),
            vm((3, 144, 384), BF16), vm((3, 144, 384), BF16),
            vm((256, 128), BF16), vm((32, 1024), BF16), vm((48, 1024), BF16),
            vm((64, 1024), BF16), vm((512, 128), BF16), vm((1024, 256), BF16),
            vm((2, 32, 1024), BF16), vm((128, 128), BF16), vm((1024, 128), BF16), vm((8, 48, 128), BF16),
            vm((48, 1024), BF16), vm((1024, 128), BF16), vm((288, 1024), BF16), vm((144, 1024), BF16),
            vm((480, 128), BF16), vm((256, 128), BF16), vm((256, 128), BF16), vm((16, 16, 128), BF16),
            vm((16, 128), BF16), vm((256, 128), BF16), vm((2, 2, 896, 128), BF16),
            vm((128, 128), F32), vm((16, 8, 128), F32), vm((8, 128), F32), vm((8, 128), F32),
            vm((128, 128), F32), vm((8, 128), F32), vm((1024, 128), BF16),
            dma((5,)), dma((5,)), dma((11, 8)), dma((11, 8)), dma((4, 16)), dma((4, 16)), dma((3, 4)), dma((3, 4)), dma((5,)),
        ],
        compiler_params=pltpu.CompilerParams(
            collective_id=0, has_side_effects=True, vmem_limit_bytes=32 * 1024 * 1024
        ),
    )(
        *(
            pltpu.with_memory_space_constraint(x, pltpu.HBM)
            for x in (
                features.reshape(128, 256),
                projection,
                first_kernel.reshape(2304, 128),
                second_kernel.reshape(1152, 128),
                cotangent.reshape(128, 128),
            )
        )
    )
    out, grad, proj_grad, first, second = pl.pallas_call(
        finish_kernel,
        out_shape=(
            jax.ShapeDtypeStruct((128, 128), BF16),
            jax.ShapeDtypeStruct((128, 256), BF16),
            jax.ShapeDtypeStruct((256, 512), F32),
            jax.ShapeDtypeStruct((2304, 128), F32),
            jax.ShapeDtypeStruct((1152, 128), F32),
        ),
        in_specs=[pl.BlockSpec(memory_space=vm)] * 4,
        out_specs=[pl.BlockSpec(memory_space=vm)] * 5,
        compiler_params=pltpu.CompilerParams(vmem_limit_bytes=16 * 1024 * 1024),
    )(out, grad, weights, proj_grad)
    return (
        out.reshape(1, 128, 128),
        grad.reshape(1, 128, 256),
        proj_grad,
        first.reshape(3, 3, 256, 128),
        second.reshape(3, 3, 128, 128),
    )


def solution(mesh):
    placed = (P("rows", "cols", None), P(), P(), P(), P("rows", "cols", None))
    return jax.shard_map(
        body,
        mesh=mesh,
        in_specs=placed,
        out_specs=(P("rows", "cols", None), P("rows", "cols", None), P(), P(), P()),
        check_vma=False,
    )
```

```python
import math

import jax
import jax.numpy as jnp
from jax import lax
from jax.experimental import pallas as pl
from jax.experimental.pallas import tpu as pltpu
from jax.sharding import PartitionSpec as P

MESH = pl.DeviceIdType.MESH
F32 = jnp.float32
BF16 = jnp.bfloat16
HEIGHT = 32
WIDTH = 1024


def remote(src, dst, send_sem, recv_sem, device):
    return pltpu.make_async_remote_copy(
        src_ref=src, dst_ref=dst, send_sem=send_sem, recv_sem=recv_sem,
        device_id=device, device_id_type=MESH,
    )


def at(start, size, align):
    return pl.ds(pl.multiple_of(start, align), size)


def dot(a, b):
    return jnp.dot(a, b, preferred_element_type=F32)


def dot_nt(a, b):
    return lax.dot_general(a, b, (((1,), (1,)), ((), ())), preferred_element_type=F32)


def dot_tn(a, b):
    return lax.dot_general(a, b, (((0,), (0,)), ((), ())), preferred_element_type=F32)


def shifted(x):
    return pltpu.roll(x, 1, 0), x, pltpu.roll(x, 143, 0)


def wait_all(copies):
    for cp in copies:
        cp.wait()


def block_kernel(
    feat_in, proj_in, k1_in, k2_in, cot_in, out_ref, ig_ref, w_out, p_out,
    feat, proj, k1, k2, cot,
    qkv_send, qkv, att_t, inv_ref, s_ref, e_ref, d_ref, kmat, vext, vext_t,
    att_send, att_recv, attx, imc, cot_l, cot_r, cotx, cim, k2t, k1t, tc,
    hx, sx, up_send, up_t, u_ext, g_t, g_recv, featx,
    att_near, slope_own, slope_row, hid_send, hid_row, cot_row, a9, h9,
    wsend, wcore, whalf, wrow, wfin, wrgat, wgat,
    pblock, prow, pfin, pcore, prgat, pmine, pgat,
    core_s, core_r, col_s, col_r, row_s, row_r, halo_s, halo_r, load_s,
):
    r = lax.axis_index("rows")
    c = lax.axis_index("cols")
    core = r % 2
    k = r // 2
    partner = (r + 1 - 2 * core, c)

    def col_dev(d):
        return (r, (c + d) % 8)

    def row_dev(d):
        return (2 * ((k + d) % 16) + core, c)

    def near(d):
        return ((r + d + 32) % 32, c)

    def to_cols(kind, src_of, dst):
        copies = []
        for d in range(1, 8):
            cp = remote(src_of((c + d) % 8), dst(d), col_s.at[kind, d], col_r.at[kind, d], col_dev(d))
            cp.start()
            copies.append(cp)
        return copies

    def to_rows(kind, src_of, dst):
        copies = []
        for d in range(1, 16):
            cp = remote(src_of((k + d) % 16), dst(d), row_s.at[kind, d], row_r.at[kind, d], row_dev(d))
            cp.start()
            copies.append(cp)
        return copies

    def to_near(kind, src, slots):
        copies = []
        for n, d in enumerate((-1, 1, -2, 2)):
            cp = remote(src, slots.at[2 - d], halo_s.at[kind, n], halo_r.at[kind, n], near(d))
            cp.start()
            copies.append(cp)
        return copies

    barrier = pltpu.get_barrier_semaphore()
    pl.semaphore_signal(barrier, inc=1, device_id=partner, device_id_type=MESH)
    pl.semaphore_signal(barrier, inc=1, device_id=near(2 * core - 1), device_id_type=MESH)
    for d in range(1, 8):
        pl.semaphore_signal(barrier, inc=1, device_id=col_dev(d), device_id_type=MESH)
    for d in range(1, 16):
        pl.semaphore_signal(barrier, inc=1, device_id=row_dev(d), device_id_type=MESH)

    loads = []
    for n, (src, dst) in enumerate(
        ((feat_in, feat), (proj_in, proj), (cot_in, cot), (k2_in, k2), (k1_in, k1))
    ):
        cp = pltpu.make_async_copy(src, dst, load_s.at[n])
        cp.start()
        loads.append(cp)

    wait_all(loads[0:2])
    packed = jnp.transpose(dot(feat[...], proj[...])).astype(BF16)
    for h in range(8):
        qkv_send[64 * h : 64 * h + 16, :] = packed[16 * h : 16 * h + 16]
        qkv_send[64 * h + 16 : 64 * h + 32, :] = packed[128 + 16 * h : 144 + 16 * h]
        qkv_send[64 * h + 32 : 64 * h + 64, :] = packed[256 + 32 * h : 288 + 32 * h]
    wait_all(loads[2:5])
    pl.semaphore_wait(barrier, 24)
    my_lanes = at(128 * c, 128, 128)
    qkv_copies = to_cols(
        0, lambda j: qkv_send.at[at(64 * j, 64, 64), :], lambda d: qkv.at[:, my_lanes]
    )
    left = remote(cot.at[112:128], cot_l, halo_s.at[2, 0], halo_r.at[2, 0], col_dev(1))
    left.start()
    right = remote(cot.at[0:16], cot_r, halo_s.at[2, 1], halo_r.at[2, 1], col_dev(7))
    right.start()
    qkv[:, my_lanes] = qkv_send[at(64 * c, 64, 64), :]
    for a in range(3):
        for b in range(3):
            n = 3 * a + b
            k2t[a, 128 * b : 128 * b + 128, :] = jnp.transpose(
                k2[128 * n : 128 * n + 128, :].astype(F32)
            ).astype(BF16)
            k1t[a, 128 * b : 128 * b + 128, :] = jnp.transpose(
                k1[256 * n : 256 * n + 256, :].astype(F32)
            ).astype(BF16)
    index = lax.broadcasted_iota(jnp.int32, (144, 128), 0)
    low_end = 136 - 8 * (c // 7)
    high_start = 136 + 8 * ((7 - c) // 7)

    def in_image(row):
        return jnp.where((row >= 0) & (row < HEIGHT), 1, 0)

    left.wait()
    right.wait()
    cotx[2] = jnp.where(
        (index < low_end) | (index >= high_start),
        jnp.concatenate([cot[...].astype(F32), cot_r[0:8, :].astype(F32), cot_l[8:16, :].astype(F32)]),
        0.0,
    ).astype(BF16)
    cot_copies = to_near(0, cotx.at[2], cotx)
    wait_all(qkv_copies)
    cot_row_copies = to_cols(8, lambda j: cot, lambda d: cot_row.at[at(128 * c, 128, 128), :])
    cot_row[at(128 * c, 128, 128), :] = cot[...]

    kmat[...] = (jnp.transpose(qkv[16:32, :].astype(F32)) * 0.25).astype(BF16)
    vext_t[0:32, :] = qkv[32:64, :]
    extra = lax.broadcasted_iota(jnp.int32, (16, 1024), 0)
    vext_t[32:48, :] = jnp.where(extra < 2, 1.0, 0.0).astype(BF16)
    vext[...] = jnp.transpose(vext_t[...].astype(F32)).astype(BF16)
    lane = lax.broadcasted_iota(jnp.int32, (32, 128), 1)
    zero = jnp.zeros((32, 128), F32)

    def send_attended(j):
        after = att_t[:, 128 * j + 128 : 128 * j + 256].astype(F32) if j < 7 else zero
        before = att_t[:, 128 * j - 128 : 128 * j].astype(F32) if j > 0 else zero
        att_send[j, :, 0:128] = att_t[:, 128 * j : 128 * j + 128]
        att_send[j, :, 128:256] = jnp.where(lane < 64, after, before).astype(BF16)

        @pl.when(c != j)
        def _():
            d = (j - c + 8) % 8
            remote(
                att_send.at[j], att_recv.at[at(32 * c, 32, 32), :], col_s.at[2, d], col_r.at[2, d], (r, j)
            ).start()

    def score(ib, jc, top):
        s = dot(kmat[128 * jc : 128 * jc + 128, :], qkv[0:16, 256 * ib : 256 * ib + 256])
        s_ref[ib % 2, 128 * jc : 128 * jc + 128, :] = s
        part = jnp.max(s.reshape(16, 8, 256), axis=0)
        return part if top is None else jnp.maximum(top, part)

    top_next = None
    for jc in range(8):
        top_next = score(0, jc, top_next)
    for ib in range(4):
        lanes = slice(256 * ib, 256 * ib + 256)
        top = jnp.max(top_next, axis=0, keepdims=True)
        top_next = None
        for jc in range(8):
            rows = slice(128 * jc, 128 * jc + 128)
            if ib < 3:
                top_next = score(ib + 1, jc, top_next)
            e_ref[rows, lanes] = jnp.exp(s_ref[ib % 2, rows, :] - top).astype(BF16)
        weighted = dot(vext_t[...], e_ref[:, lanes])
        inverse = 1.0 / weighted[32:33, :]
        inv_ref[0:1, lanes] = inverse
        att_t[:, lanes] = (weighted[0:32, :] * inverse).astype(BF16)
        for j in ((0,), (1, 2), (3, 4), (5, 6, 7))[ib]:
            send_attended(j)

    row_copies = []
    for n, d in enumerate((-1, 1)):
        cp = remote(att_t, att_near.at[n], halo_s.at[2, 2 + n], halo_r.at[2, 2 + n], near(d))
        cp.start()
        row_copies.append(cp)
    att_recv[at(32 * c, 32, 32), :] = att_send[c]

    wait_all(cot_copies)
    for slot in range(5):
        x = cotx[slot].astype(F32) * in_image(r - 2 + slot).astype(F32)
        low, mid, high = shifted(x)
        cim[slot, :, 0:128] = high.astype(BF16)
        cim[slot, :, 128:256] = mid.astype(BF16)
        cim[slot, :, 256:384] = low.astype(BF16)
    for t in range(3):
        tc[t] = (
            dot(cim[t + 2], k2t[0]) + dot(cim[t + 1], k2t[1]) + dot(cim[t], k2t[2])
        )

    for d in range(1, 8):
        remote(
            att_send.at[(c + d) % 8], att_recv.at[at(32 * c, 32, 32), :],
            col_s.at[2, d], col_r.at[2, d], col_dev(d),
        ).wait()
    turned = jnp.transpose(att_recv[...].astype(F32))
    attx[2] = jnp.concatenate([turned[0:136], turned[248:256]]).astype(BF16)
    near_copies = to_near(1, attx.at[2], attx)

    def columns(slot):
        x = attx[slot].astype(F32) * in_image(r - 2 + slot).astype(F32)
        low, mid, high = shifted(x)
        imc[slot, :, 0:256] = low.astype(BF16)
        imc[slot, :, 256:512] = mid.astype(BF16)
        imc[slot, :, 512:768] = high.astype(BF16)

    columns(2)
    column = lax.broadcasted_iota(jnp.int32, (48, 1024), 1)

    def lane_shifted(x):
        n = x.shape[0]
        low = jnp.where(column[0:n] == 0, 0.0, pltpu.roll(x, 1, 1))
        high = jnp.where(column[0:n] == 1023, 0.0, pltpu.roll(x, 1023, 1))
        return low.astype(BF16), x.astype(BF16), high.astype(BF16)

    wait_all(row_copies)
    for a in range(3):
        x = (att_near[1], att_t[...], att_near[0])[a].astype(F32) * in_image(r - 1 + a).astype(F32)
        for b, y in enumerate(lane_shifted(x)):
            a9[96 * a + 32 * b : 96 * a + 32 * b + 32, :] = y
    wait_all(near_copies[0:2])
    columns(1)
    columns(3)

    for t in (1, 0, 2):
        if t == 0:
            wait_all(near_copies[2:4])
            columns(0)
            columns(4)
        pre = (
            dot(imc[t], k1[0:768, :])
            + dot(imc[t + 1], k1[768:1536, :])
            + dot(imc[t + 2], k1[1536:2304, :])
        )
        valid = in_image(r - 1 + t)
        keep = (index < low_end * valid) | (index >= 144 - (144 - high_start) * valid)
        sigma = 1.0 / (1.0 + jnp.exp(-pre))
        slope = jnp.where(keep, tc[t] * (sigma * (1.0 + pre * (1.0 - sigma))), 0.0)
        low, mid, high = shifted(slope)
        sx[t, :, 0:128] = high.astype(BF16)
        sx[t, :, 128:256] = mid.astype(BF16)
        sx[t, :, 256:384] = low.astype(BF16)
        if t == 1:
            slope_own[...] = slope[0:128].astype(BF16)
            slope_copies = to_cols(4, lambda j: slope_own, lambda d: slope_row.at[at(128 * c, 128, 128), :])
        hidden = jnp.where(keep, pre * sigma, 0.0)
        low, mid, high = shifted(hidden)
        hx[t, :, 0:128] = low.astype(BF16)
        hx[t, :, 128:256] = mid.astype(BF16)
        hx[t, :, 256:384] = high.astype(BF16)

    upstream = (
        dot(sx[2, 0:128, :], k1t[0]) + dot(sx[1, 0:128, :], k1t[1]) + dot(sx[0, 0:128, :], k1t[2])
    )
    up_send[...] = jnp.transpose(upstream).astype(BF16)
    up_copies = to_cols(3, lambda j: up_send.at[at(32 * j, 32, 32), :], lambda d: up_t.at[:, my_lanes])
    up_t[:, my_lanes] = up_send[at(32 * c, 32, 32), :]

    for t in range(3):
        turned = jnp.transpose(hx[t, 0:128, 128:256].astype(F32)).astype(BF16)
        for j in range(8):
            hid_send[j, 16 * t : 16 * t + 16, :] = turned[16 * j : 16 * j + 16]
    hid_copies = to_cols(5, lambda j: hid_send.at[j], lambda d: hid_row.at[:, my_lanes])
    feat_copies = to_cols(1, lambda j: feat, lambda d: featx.at[at(128 * c, 128, 128), :])
    featx[at(128 * c, 128, 128), :] = feat[...]
    slope_row[at(128 * c, 128, 128), :] = slope_own[...]
    hid_row[:, my_lanes] = hid_send[c]
    out_ref[...] = (
        dot(hx[0, 0:128, :], k2[0:384, :])
        + dot(hx[1, 0:128, :], k2[384:768, :])
        + dot(hx[2, 0:128, :], k2[768:1152, :])
    ).astype(BF16)

    wait_all(up_copies)
    scaled = (up_t[...].astype(F32) * inv_ref[0:1, :]).astype(BF16)
    u_ext[0:32, :] = scaled
    inner = jnp.sum(scaled.astype(F32) * att_t[...].astype(F32), axis=0, keepdims=True)
    inner_high = inner.astype(BF16).astype(F32)
    extra = lax.broadcasted_iota(jnp.int32, (16, 1024), 0)
    u_ext[32:48, :] = jnp.where(
        extra == 0, -inner_high, jnp.where(extra == 1, inner_high - inner, 0.0)
    ).astype(BF16)

    def backward(ib):
        lanes = slice(256 * ib, 256 * ib + 256)
        u_block = u_ext[:, lanes]
        for jc in range(8):
            rows = slice(128 * jc, 128 * jc + 128)
            slopes = dot(vext[rows, :], u_block)
            d_ref[rows, lanes] = (e_ref[rows, lanes].astype(F32) * slopes).astype(BF16)
        g_t[0:16, lanes] = (dot(qkv[16:32, :], d_ref[:, lanes]) * 0.25).astype(BF16)

    wait_all(slope_copies)
    wait_all(cot_row_copies)
    wait_all(hid_copies)
    wsend[0:288, :] = dot(a9[...], slope_row[...]).astype(BF16)
    for b, y in enumerate(lane_shifted(hid_row[...].astype(F32))):
        for a in range(3):
            h9[48 * a + 16 * b : 48 * a + 16 * b + 16, :] = y[16 * a : 16 * a + 16]
    wsend[288:432, :] = dot(h9[...], cot_row[...]).astype(BF16)
    wsend[432:480, :] = jnp.zeros((48, 128), BF16)
    w_copy = remote(wsend.at[at(224 * (1 - core), 256, 32)], wcore, core_s.at[0], core_r.at[0], partner)
    w_copy.start()

    backward(0)
    backward(1)
    w_copy.wait()
    whalf[...] = (wsend[at(224 * core, 256, 32), :].astype(F32) + wcore[...].astype(F32)).astype(BF16)
    w_copies = to_rows(1, lambda j: whalf.at[at(16 * j, 16, 16), :], lambda d: wrow.at[d])
    backward(2)
    backward(3)

    g_t[32:64, :] = dot_nt(u_ext[0:32, :], e_ref[...]).astype(BF16)
    g_t[16:32, :] = (dot_nt(qkv[0:16, :], d_ref[...]) * 0.25).astype(BF16)


    wait_all(feat_copies)
    turned = dot(g_t[...], featx[...])
    pblock[0:64, :] = turned[:, 0:128]
    pblock[64:128, :] = turned[:, 128:256]
    p2 = to_rows(0, lambda j: pblock.at[at(8 * j, 8, 8), :], lambda d: prow.at[d])
    g_copies = to_cols(6, lambda j: g_t.at[:, at(128 * j, 128, 128)], lambda d: g_recv.at[at(64 * c, 64, 64), :])
    g_recv[at(64 * c, 64, 64), :] = g_t[:, my_lanes]

    wait_all(p2)
    total = pblock[at(8 * k, 8, 8), :]
    for d in range(1, 16):
        total = total + prow[d]
    pfin[...] = total
    p3 = remote(pfin, pcore, core_s.at[2], core_r.at[2], partner)
    p3.start()
    wait_all(w_copies)
    total = whalf[at(16 * k, 16, 16), :].astype(F32)
    for d in range(1, 16):
        total = total + wrow[d].astype(F32)
    wfin[...] = total.astype(BF16)
    wrgat[at(16 * k, 16, 16), :] = wfin[...]
    w_copies = to_rows(2, lambda j: wfin, lambda d: wrgat.at[at(16 * k, 16, 16), :])
    p3.wait()
    pmine[...] = pfin[...] + pcore[...]
    p4 = to_rows(3, lambda j: pmine, lambda d: prgat.at[at(8 * k, 8, 8), :])
    prgat[at(8 * k, 8, 8), :] = pmine[...]
    wait_all(w_copies)
    back = []
    for m in range(2):
        place = at(112 * c, 112, 16)
        wgat[core, m, place, :] = wrgat[112 * m : 112 * m + 112, :]
        back.append(to_cols(7 if m == 0 else 10, lambda j: wgat.at[core, m, place, :], lambda d: wgat.at[core, m, place, :]))
    wait_all(g_copies)
    parts = []
    for first, size in ((0, 16), (16, 16), (32, 32)):
        for h in range(8):
            parts.append(g_recv[64 * h + first : 64 * h + first + size, :].astype(F32))
    grads = jnp.transpose(jnp.concatenate(parts)).astype(BF16)
    ig_ref[...] = dot_nt(grads, proj[...]).astype(BF16)

    wait_all(p4)
    pgat[at(128 * c, 128, 128), :] = prgat[...].astype(BF16)
    block = pgat.at[at(128 * c, 128, 128), :]
    p5 = to_cols(9, lambda j: block, lambda d: block)
    swap = []
    for m in range(2):
        wait_all(back[m])
        cp = remote(wgat.at[core, m], wgat.at[core, m], core_s.at[3 + m], core_r.at[3 + m], partner)
        cp.start()
        swap.append(cp)
    wait_all(p5)
    for h in range(8):
        for side in range(2):
            base = 128 * h + 64 * side
            lanes = slice(128 * side, 128 * side + 128)
            p_out[16 * h : 16 * h + 16, lanes] = pgat[base : base + 16, :]
            p_out[128 + 16 * h : 144 + 16 * h, lanes] = pgat[base + 16 : base + 32, :]
            p_out[256 + 32 * h : 288 + 32 * h, lanes] = pgat[base + 32 : base + 64, :]
    for cp in swap:
        cp.wait()
    w_out[...] = wgat[...]


def finish_kernel(out_in, ig_in, w_in, p_in, out_ref, ig_ref, proj_ref, first_ref, second_ref):
    factor = 1.0 / math.sqrt(HEIGHT * WIDTH)
    out_ref[...] = out_in[...]
    ig_ref[...] = ig_in[...]
    proj_ref[...] = jnp.transpose(p_in[...].astype(F32)) * factor
    for h in range(8):
        for n in range(27):
            q, row = n // 7, 112 * h + 16 * (n % 7)
            values = w_in[q // 2, q % 2, row : row + 16, :].astype(F32) * factor
            if n < 18:
                start = 256 * (n // 2) + 32 * h + 16 * (n % 2)
                first_ref[start : start + 16, :] = values
            else:
                start = 128 * (n - 18) + 16 * h
                second_ref[start : start + 16, :] = values


def body(features, projection, first_kernel, second_kernel, cotangent):
    vm = pltpu.VMEM
    dma = pltpu.SemaphoreType.DMA
    out, grad, weights, proj_grad = pl.pallas_call(
        block_kernel,
        out_shape=(
            jax.ShapeDtypeStruct((128, 128), BF16),
            jax.ShapeDtypeStruct((128, 256), BF16),
            jax.ShapeDtypeStruct((2, 2, 896, 128), BF16),
            jax.ShapeDtypeStruct((512, 256), BF16),
        ),
        in_specs=[pl.BlockSpec(memory_space=pltpu.HBM)] * 5,
        out_specs=[pl.BlockSpec(memory_space=vm)] * 4,
        scratch_shapes=[
            vm((128, 256), BF16), vm((256, 512), BF16), vm((2304, 128), BF16), vm((1152, 128), BF16), vm((128, 128), BF16),
            vm((512, 128), BF16), vm((64, 1024), BF16), vm((32, 1024), BF16), vm((8, 1024), F32),
            vm((2, 1024, 256), F32), vm((1024, 1024), BF16), vm((1024, 1024), BF16),
            vm((1024, 16), BF16), vm((1024, 48), BF16), vm((48, 1024), BF16),
            vm((8, 32, 256), BF16), vm((256, 256), BF16), vm((5, 144, 256), BF16), vm((5, 144, 768), BF16),
            vm((16, 128), BF16), vm((16, 128), BF16), vm((5, 144, 128), BF16), vm((5, 144, 384), BF16),
            vm((3, 384, 128), BF16), vm((3, 384, 256), BF16), vm((3, 144, 128), F32),
            vm((3, 144, 384), BF16), vm((3, 144, 384), BF16),
            vm((256, 128), BF16), vm((32, 1024), BF16), vm((48, 1024), BF16),
            vm((64, 1024), BF16), vm((512, 128), BF16), vm((1024, 256), BF16),
            vm((2, 32, 1024), BF16), vm((128, 128), BF16), vm((1024, 128), BF16), vm((8, 48, 128), BF16),
            vm((48, 1024), BF16), vm((1024, 128), BF16), vm((288, 1024), BF16), vm((144, 1024), BF16),
            vm((480, 128), BF16), vm((256, 128), BF16), vm((256, 128), BF16), vm((16, 16, 128), BF16),
            vm((16, 128), BF16), vm((256, 128), BF16), vm((2, 2, 896, 128), BF16),
            vm((128, 128), F32), vm((16, 8, 128), F32), vm((8, 128), F32), vm((8, 128), F32),
            vm((128, 128), F32), vm((8, 128), F32), vm((1024, 128), BF16),
            dma((5,)), dma((5,)), dma((11, 8)), dma((11, 8)), dma((4, 16)), dma((4, 16)), dma((3, 4)), dma((3, 4)), dma((5,)),
        ],
        compiler_params=pltpu.CompilerParams(
            collective_id=0, has_side_effects=True, vmem_limit_bytes=32 * 1024 * 1024
        ),
    )(
        *(
            pltpu.with_memory_space_constraint(x, pltpu.HBM)
            for x in (
                features.reshape(128, 256),
                projection,
                first_kernel.reshape(2304, 128),
                second_kernel.reshape(1152, 128),
                cotangent.reshape(128, 128),
            )
        )
    )
    out, grad, proj_grad, first, second = pl.pallas_call(
        finish_kernel,
        out_shape=(
            jax.ShapeDtypeStruct((128, 128), BF16),
            jax.ShapeDtypeStruct((128, 256), BF16),
            jax.ShapeDtypeStruct((256, 512), F32),
            jax.ShapeDtypeStruct((2304, 128), F32),
            jax.ShapeDtypeStruct((1152, 128), F32),
        ),
        in_specs=[pl.BlockSpec(memory_space=vm)] * 4,
        out_specs=[pl.BlockSpec(memory_space=vm)] * 5,
        compiler_params=pltpu.CompilerParams(vmem_limit_bytes=16 * 1024 * 1024),
    )(out, grad, weights, proj_grad)
    return (
        out.reshape(1, 128, 128),
        grad.reshape(1, 128, 256),
        proj_grad,
        first.reshape(3, 3, 256, 128),
        second.reshape(3, 3, 128, 128),
    )


def solution(mesh):
    placed = (P("rows", "cols", None), P(), P(), P(), P("rows", "cols", None))
    return jax.shard_map(
        body,
        mesh=mesh,
        in_specs=placed,
        out_specs=(P("rows", "cols", None), P("rows", "cols", None), P(), P(), P()),
        check_vma=False,
    )
```
